512 devices in a mesh: rows: 128 (over z, x, core), grp: 4 (over y).
Axes of the slice: x: 4, y: 4, z: 16, core: 2. Of those that a mesh axis runs over, the one named last changes fastest.
Arguments:
- features: bfloat16 [4, 196608, 128], P('grp', 'rows'), may hold values from -6 to 6
- length_scale: bfloat16 [4, 196608], P('grp', 'rows'), may hold values from 32 to 256
- prior: bfloat16 [4, 196608], P('grp', 'rows'), may hold values from 0.45 to 18
- partners: int32 [4, 1536, 16], P('grp', 'rows'), may hold values from 0 to 1535, as said below
- counts: int32 [4, 1536], P('grp', 'rows'), may hold values from 12 to 16
- projection: bfloat16 [128, 64], replicated, may hold values from -0.5 to 0.5
Outputs:
- first_basis: float32 [4, 64, 196608], P('grp', None, 'rows')
- embedding: float32 [4, 64, 196608], P('grp', None, 'rows')
The draws below stay inside these ranges and needn't reach their ends.
Inputs may be any that keep to these rules, and one draw needn't show every extreme that they name: `partners`: slot 0 of each tile names the tile itself; slots 1 to 12 name tiles held by the same device; slots 13 onward name tiles held by other devices along rows in the same group. Tiles may repeat in a list. Over one device's tiles, slots 13 onward name tiles of any one other device at most 1 times, and exactly 1 times for some device.
All inputs are finite; a program needn't handle non-finite values.
Results may differ from the reference program's by a relative error of at most 0.0047.
Values may be sent and summed in bfloat16 or wider, within the bound.
A program may use at most 128 MiB of HBM per device.

```python
import math
import jax
import jax.numpy as jnp
from jax import lax

F = 128
C = 64
TILE = 128
PART = 16
NEAR = 13
TILES_DEV = 12
TILES_G = 1536
ROWS_G = 196608
GROUPS = 4
CAP = 1


def draw_features(key, part):
    feature_key = jax.random.fold_in(key, 11)
    values = jnp.clip(jax.random.normal(feature_key, (GROUPS, ROWS_G, F), jnp.float32), -6.0, 6.0)
    return values.astype(jnp.bfloat16)


def draw_prior(key, part):
    prior_key = jax.random.fold_in(key, 23)
    position = (jnp.arange(GROUPS, dtype=jnp.float32)[:, None] * ROWS_G + jnp.arange(ROWS_G, dtype=jnp.float32)[None, :]) / (GROUPS * ROWS_G)
    ramp = 1.0 + 2.0 * position
    values = ramp * jnp.exp(jax.random.uniform(prior_key, (GROUPS, ROWS_G), jnp.float32, -0.7, 0.7))
    return values.astype(jnp.bfloat16)


def device_lists(base_key, group_index, device_index):
    nrows = TILES_G // TILES_DEV
    far_count = TILES_DEV * (PART - NEAR)
    device_key = jax.random.fold_in(jax.random.fold_in(base_key, group_index), device_index)
    key_near, key_chosen, key_pool, key_order, key_local = jax.random.split(device_key, 5)
    own_tiles = device_index * TILES_DEV + jnp.arange(TILES_DEV, dtype=jnp.int32)
    near_tiles = device_index * TILES_DEV + jax.random.randint(key_near, (TILES_DEV, NEAR - 1), 0, TILES_DEV)
    chosen = jax.random.randint(key_chosen, (), 0, nrows - 1)
    others = jnp.arange(nrows - 2, dtype=jnp.int32)
    others = others + (others >= chosen).astype(jnp.int32)
    pool = jax.random.permutation(key_pool, jnp.repeat(others, CAP))
    sequence = jnp.concatenate([jnp.full((CAP,), chosen, jnp.int32), pool[:far_count - CAP]])
    sequence = jax.random.permutation(key_order, sequence)
    owner_device = (device_index + 1 + sequence) % nrows
    far_tiles = owner_device * TILES_DEV + jax.random.randint(key_local, (far_count,), 0, TILES_DEV)
    return jnp.concatenate([own_tiles[:, None], near_tiles, far_tiles.reshape(TILES_DEV, PART - NEAR)], axis=1).astype(jnp.int32)


def draw_partners(key, part):
    base_key = jax.random.fold_in(key, 41)
    nrows = TILES_G // TILES_DEV
    group_ids = jnp.arange(GROUPS, dtype=jnp.int32)
    device_ids = jnp.arange(nrows, dtype=jnp.int32)
    lists = jax.vmap(lambda group_index: jax.vmap(lambda device_index: device_lists(base_key, group_index, device_index))(device_ids))(group_ids)
    return lists.reshape(GROUPS, TILES_G, PART)


def draw_counts(key, part):
    count_key = jax.random.fold_in(key, 31)
    key_drop, key_spot = jax.random.split(count_key)
    values = PART - jax.random.randint(key_drop, (GROUPS, TILES_G), 0, PART - NEAR + 2)
    spot = jax.random.randint(key_spot, (GROUPS,), 0, TILES_G)
    filled = jnp.arange(TILES_G, dtype=jnp.int32)[None, :] == spot[:, None]
    return jnp.where(filled, PART, values).astype(jnp.int32)


def block_levels(key, shape, pieces, low, largest):
    loudness, own = 1.0, jax.random.fold_in(key, 6)
    for dim, blocks in pieces:
        steps = jnp.exp(jax.random.uniform(jax.random.fold_in(own, dim), (blocks,), jnp.float32, low / len(pieces), largest / len(pieces)))
        loudness = loudness * jnp.repeat(steps, shape[dim] // blocks).reshape([-1 if axis == dim else 1 for axis in range(len(shape))])
    return loudness


def noise(stream_key, extent, deviation, most, kind=jnp.bfloat16):
    entries = deviation * jax.random.normal(stream_key, extent, jnp.float32)
    return jnp.clip(entries, min=-most, max=most).astype(kind)


def setup_inputs(seed: int = 0) -> dict:
    keys = jax.random.split(jax.random.key(seed), 7)
    return {
        "features": draw_features(jax.random.fold_in(keys[6], 71), 0),
        "length_scale": jnp.clip(jnp.exp(math.log(256.0) - 2.0794415 * jax.random.uniform(keys[1], (GROUPS, ROWS_G), jnp.float32) ** block_levels(keys[1], (GROUPS, ROWS_G), ((0, 4), (1, 128)), -0.2, 0.2)), 32.0, 256.0).astype(jnp.bfloat16),
        "prior": draw_prior(jax.random.fold_in(keys[6], 71), 0),
        "partners": draw_partners(jax.random.fold_in(keys[6], 71), 0),
        "counts": draw_counts(jax.random.fold_in(keys[6], 71), 0),
        "projection": noise(keys[5], (F, C), F ** -0.5, 0.5),
    }


def kernel_tiles(own_rows, own_norm, own_band, part_rows, part_norm, part_band, alive_mask):
    cross_products = jnp.einsum('naf,nsbf->nsab', own_rows.astype(jnp.float32), part_rows.astype(jnp.float32))
    distance = jnp.maximum(own_norm[:, None, :, None] + part_norm[:, :, None, :] - 2.0 * cross_products, 0.0)
    spread = own_band.astype(jnp.float32)[:, None, :, None] + part_band.astype(jnp.float32)[:, :, None, :]
    return jnp.where(alive_mask[:, :, None, None], jnp.exp(-distance / spread), 0.0)

def density_term(kernel, extras):
    return jnp.sum(kernel, axis=(1, 3))

def walk_term(kernel, extras):
    rounded = lax.optimization_barrier(kernel.astype(jnp.bfloat16)).astype(jnp.float32)
    degree = jnp.sum(rounded * extras[0][:, :, None, :], axis=(1, 3))
    product = jnp.einsum('nsab,nscb->nca', rounded, extras[1].astype(jnp.float32))
    return (degree, product)

def apply_term(kernel, extras):
    rounded = lax.optimization_barrier(kernel.astype(jnp.bfloat16)).astype(jnp.float32)
    return jnp.einsum('nsab,nscb->nca', rounded, extras[0].astype(jnp.float32))

def orthonormal(raw_basis, total_rows):
    gram_matrix = jnp.einsum('nca,nda->cd', raw_basis, raw_basis, precision=lax.Precision.HIGHEST) / total_rows
    lower = jnp.linalg.cholesky(gram_matrix)
    identity = jnp.eye(gram_matrix.shape[0], dtype=gram_matrix.dtype)
    lower_inverse = lax.linalg.triangular_solve(lower, identity, left_side=True, lower=True)
    return jnp.einsum('dc,nca->nda', lower_inverse, raw_basis, precision=lax.Precision.HIGHEST)

def columns_first(tile_basis):
    shaped = tile_basis.reshape(GROUPS, TILES_G, C, TILE)
    return jnp.transpose(shaped, (0, 2, 1, 3)).reshape(GROUPS, C, ROWS_G)

def reference(features, length_scale, prior, partners, counts, projection):
    total_tiles = GROUPS * TILES_G
    tile_rows = features.reshape(total_tiles, TILE, F)
    tile_norm = jnp.sum(jnp.square(tile_rows.astype(jnp.float32)), axis=-1)
    tile_band = length_scale.reshape(total_tiles, TILE)
    tile_prior = prior.reshape(total_tiles, TILE).astype(jnp.float32)
    group_first = (jnp.arange(GROUPS, dtype=jnp.int32) * TILES_G)[:, None, None]
    slot_table = (partners + group_first).reshape(total_tiles, PART).astype(jnp.int32)
    alive_table = jnp.arange(PART, dtype=jnp.int32)[None, :] < counts.reshape(total_tiles, 1)
    block_count = total_tiles // TILES_DEV
    own_arrays = (tile_rows, tile_norm, tile_band)

    def sweep_blocks(block_term, extras):

        def one_block(block_step):
            first_tile = block_step * TILES_DEV
            own_block = [lax.dynamic_slice_in_dim(member, first_tile, TILES_DEV, 0) for member in own_arrays]
            slot_block = lax.dynamic_slice_in_dim(slot_table, first_tile, TILES_DEV, 0)
            alive_block = lax.dynamic_slice_in_dim(alive_table, first_tile, TILES_DEV, 0)
            gathered = [jnp.take(member, slot_block, axis=0) for member in own_arrays + extras]
            kernel = kernel_tiles(own_block[0], own_block[1], own_block[2], gathered[0], gathered[1], gathered[2], alive_block)
            return block_term(kernel, gathered[3:])
        stacked = lax.map(one_block, jnp.arange(block_count, dtype=jnp.int32))
        return jax.tree.map(lambda stacked_part: stacked_part.reshape((total_tiles,) + stacked_part.shape[2:]), stacked)
    density = sweep_blocks(density_term, ())
    inverse_density = 1.0 / density
    start_basis = jnp.einsum('naf,fc->nca', tile_rows.astype(jnp.float32), projection.astype(jnp.float32))
    start_scaled = lax.optimization_barrier((start_basis * (tile_prior * inverse_density)[:, None, :]).astype(jnp.bfloat16))
    degree, product = sweep_blocks(walk_term, (inverse_density, start_scaled))
    total_rows = GROUPS * ROWS_G
    first_basis = orthonormal(product / degree[:, None, :], total_rows)
    next_scaled = lax.optimization_barrier((first_basis * inverse_density[:, None, :]).astype(jnp.bfloat16))
    second = sweep_blocks(apply_term, (next_scaled,))
    final_basis = orthonormal(second / degree[:, None, :], total_rows)
    return (columns_first(first_basis), columns_first(final_basis))
```

```python
import functools

import jax
import jax.numpy as jnp
from jax import lax
from jax.experimental import pallas as pl
from jax.experimental.pallas import tpu as pltpu
from jax.sharding import PartitionSpec as P

NEAR = 13
PLANE = 8
MESH = pl.DeviceIdType.MESH
VMEM = pl.BlockSpec(memory_space=pltpu.VMEM)
SMEM = pl.BlockSpec(memory_space=pltpu.SMEM)


def nt_dot(left, right, precision=None):
    return lax.dot_general(
        left,
        right,
        (((1,), (1,)), ((), ())),
        precision=precision,
        preferred_element_type=jnp.float32,
    )


def slot_tile(table, tile, slot, slots, tiles):
    if slot < NEAR:
        return table[tile * slots + slot]
    return tiles + tile * (slots - NEAR) + (slot - NEAR)


def kernel_body(tiles, slots, table, counts, pool, band, kernel_half, inverse, norm_b, band_b, norm_a):
    size = pool.shape[1]

    def prepare(index, carry):
        rows = pool[index].astype(jnp.float32)
        norm = jnp.sum(rows * rows, axis=1, keepdims=True)
        wide = jnp.broadcast_to(-norm, (size, size))
        norm_b[index] = wide
        band_b[index] = jnp.transpose(jnp.broadcast_to(band[index], (size, size)))

        @pl.when(index < tiles)
        def _():
            norm_a[index] = jnp.transpose(wide)[0:1, :]

        return carry

    lax.fori_loop(0, pool.shape[0], prepare, 0)

    def one_tile(tile, carry):
        doubled = pool[tile] * jnp.bfloat16(2)
        own_norm = norm_a[tile]
        own_band = band[tile]
        live = counts[tile]
        total = jnp.zeros((8, size), jnp.float32)
        for slot in range(slots):
            index = slot_tile(table, tile, slot, slots, tiles)
            cross = nt_dot(pool[index], doubled)
            level = jnp.minimum(cross + (norm_b[index] + own_norm), 0.0)
            value = jnp.exp(level / (band_b[index] + own_band))
            if slot >= NEAR - 1:
                value = jnp.where(slot < live, value, 0.0)
            kernel_half[tile, slot] = value.astype(jnp.bfloat16)
            total = total + jnp.sum(value.reshape(size // 8, 8, size), axis=0)
        inverse[tile] = 1.0 / jnp.sum(total, axis=0, keepdims=True)
        return carry

    lax.fori_loop(0, tiles, one_tile, 0)


def build_kernel(table, counts, pool, band, tiles, slots):
    count, size, _ = pool.shape
    return pl.pallas_call(
        functools.partial(kernel_body, tiles, slots),
        out_shape=(
            jax.ShapeDtypeStruct((tiles, slots, size, size), jnp.bfloat16),
            jax.ShapeDtypeStruct((tiles, 1, size), jnp.float32),
        ),
        in_specs=[SMEM, SMEM, VMEM, VMEM],
        out_specs=(VMEM, VMEM),
        scratch_shapes=[
            pltpu.VMEM((count, size, size), jnp.float32),
            pltpu.VMEM((count, size, size), jnp.float32),
            pltpu.VMEM((tiles, 1, size), jnp.float32),
        ],
        name="kernel_density",
    )(table, counts, pool, band)


def walk_body(
    tiles, slots, table, pool, prior, inverse, projection, kernel_half, raw, degree, gram, scaled
):
    size = pool.shape[1]
    columns = projection.shape[0]

    def prepare(index, carry):
        start = nt_dot(projection[...], pool[index])
        inv = inverse[index]
        scaled[index, 0:columns, :] = (start * (prior[index] * inv)).astype(jnp.bfloat16)
        high = inv.astype(jnp.bfloat16).astype(jnp.float32)
        row = lax.broadcasted_iota(jnp.int32, (16, size), 0)
        extra = jnp.where(row == 0, high, jnp.where(row == 1, inv - high, 0.0))
        scaled[index, columns : columns + 16, :] = extra.astype(jnp.bfloat16)
        return carry

    lax.fori_loop(0, pool.shape[0], prepare, 0)
    gram[...] = jnp.zeros_like(gram)

    def one_tile(tile, carry):
        total = jnp.zeros((columns + 16, size), jnp.float32)
        for slot in range(slots):
            index = slot_tile(table, tile, slot, slots, tiles)
            total = total + jnp.dot(
                scaled[index], kernel_half[tile, slot], preferred_element_type=jnp.float32
            )
        below = total[columns : columns + 1] + total[columns + 1 : columns + 2]
        degree[tile] = below
        value = total[0:columns] / below
        raw[:, pl.ds(pl.multiple_of(tile * size, size), size)] = value
        gram[...] += nt_dot(value, value, lax.Precision.HIGHEST)
        return carry

    lax.fori_loop(0, tiles, one_tile, 0)


def first_walk(table, pool, prior, inverse, projection, kernel_half):
    tiles, slots, size, _ = kernel_half.shape
    columns = projection.shape[0]
    return pl.pallas_call(
        functools.partial(walk_body, tiles, slots),
        out_shape=(
            jax.ShapeDtypeStruct((columns, tiles * size), jnp.float32),
            jax.ShapeDtypeStruct((tiles, 1, size), jnp.float32),
            jax.ShapeDtypeStruct((columns, columns), jnp.float32),
        ),
        in_specs=[SMEM, VMEM, VMEM, VMEM, VMEM, VMEM],
        out_specs=(VMEM, VMEM, VMEM),
        scratch_shapes=[pltpu.VMEM((pool.shape[0], columns + 16, size), jnp.bfloat16)],
        name="first_walk",
    )(table, pool, prior, inverse, projection, kernel_half)


def basis_body(tiles, lower_inverse, raw, inverse, basis, scaled):
    size = inverse.shape[2]
    value = jnp.dot(
        lower_inverse[...],
        raw[...],
        precision=lax.Precision.HIGHEST,
        preferred_element_type=jnp.float32,
    )
    basis[...] = value
    for tile in range(tiles):
        part = value[:, tile * size : (tile + 1) * size]
        scaled[tile] = (part * inverse[tile]).astype(jnp.bfloat16)


def first_basis_of(lower_inverse, raw, inverse):
    tiles, _, size = inverse.shape
    columns = raw.shape[0]
    return pl.pallas_call(
        functools.partial(basis_body, tiles),
        out_shape=(
            jax.ShapeDtypeStruct(raw.shape, jnp.float32),
            jax.ShapeDtypeStruct((tiles, columns, size), jnp.bfloat16),
        ),
        in_specs=[VMEM, VMEM, VMEM],
        out_specs=(VMEM, VMEM),
        name="first_basis",
    )(lower_inverse, raw, inverse)


def apply_body(tiles, slots, table, own, far, degree, kernel_half, raw, gram):
    size = own.shape[2]
    columns = own.shape[1]
    gram[...] = jnp.zeros_like(gram)

    def one_tile(tile, carry):
        total = jnp.zeros((columns, size), jnp.float32)
        for slot in range(slots):
            if slot < NEAR:
                left = own[table[tile * slots + slot]]
            else:
                left = far[tile * (slots - NEAR) + (slot - NEAR)]
            total = total + jnp.dot(
                left, kernel_half[tile, slot], preferred_element_type=jnp.float32
            )
        value = total / degree[tile]
        raw[:, pl.ds(pl.multiple_of(tile * size, size), size)] = value
        gram[...] += nt_dot(value, value, lax.Precision.HIGHEST)
        return carry

    lax.fori_loop(0, tiles, one_tile, 0)


def second_walk(table, own, far, degree, kernel_half):
    tiles, slots, size, _ = kernel_half.shape
    columns = own.shape[1]
    return pl.pallas_call(
        functools.partial(apply_body, tiles, slots),
        out_shape=(
            jax.ShapeDtypeStruct((columns, tiles * size), jnp.float32),
            jax.ShapeDtypeStruct((columns, columns), jnp.float32),
        ),
        in_specs=[SMEM, VMEM, VMEM, VMEM, VMEM],
        out_specs=(VMEM, VMEM),
        name="second_walk",
    )(table, own, far, degree, kernel_half)


def reduce_body(nz, ny, local, out, parts_w, parts_y, parts_z, stage, sw, rw, sy, ry, sz, rz, sa, ra):
    row = lax.axis_index("rows")
    y = lax.axis_index("grp")
    w = row % PLANE
    z = row // PLANE

    def peer_w(step):
        other = (w + step) % PLANE
        return other, (z * PLANE + other, y)

    def peer_y(step):
        other = (y + step) % ny
        return other, (row, other)

    def peer_z(step):
        other = (z + step) % nz
        return other, (other * PLANE + w, y)

    barrier = pltpu.get_barrier_semaphore()
    for count, peer in ((PLANE, peer_w), (ny, peer_y), (nz, peer_z)):

        def greet(step, carry):
            pl.semaphore_signal(barrier, inc=1, device_id=peer(step)[1], device_id_type=MESH)
            return carry

        lax.fori_loop(1, count, greet, 0)
    pl.semaphore_wait(barrier, PLANE + ny + nz - 3)

    def exchange(count, peer, me, source, target, send, recv):
        def copy(step, mine):
            other, device = peer(step)
            return pltpu.make_async_remote_copy(
                src_ref=source(other),
                dst_ref=target.at[me if mine else other],
                send_sem=send.at[other],
                recv_sem=recv.at[me if mine else other],
                device_id=device,
                device_id_type=MESH,
            )

        def start(step, carry):
            copy(step, True).start()
            return carry

        def finish(step, carry):
            copy(step, True).wait_send()
            copy(step, False).wait_recv()
            return carry

        lax.fori_loop(1, count, start, 0)
        lax.fori_loop(1, count, finish, 0)

    exchange(PLANE, peer_w, w, lambda other: local.at[other], parts_w, sw, rw)
    parts_w[w] = local[w]
    stage[0] = jnp.sum(parts_w[...], axis=0)
    exchange(ny, peer_y, y, lambda other: stage.at[0], parts_y, sy, ry)
    parts_y[y] = stage[0]
    stage[1] = jnp.sum(parts_y[...], axis=0)
    exchange(nz, peer_z, z, lambda other: stage.at[1], parts_z, sz, rz)
    parts_z[z] = stage[1]
    stage[2] = jnp.sum(parts_z[...], axis=0)
    exchange(PLANE, peer_w, w, lambda other: stage.at[2], out, sa, ra)
    out[w] = stage[2]


def total_gram(gram):
    columns = gram.shape[0]
    height = columns // PLANE
    ny = lax.axis_size("grp")
    nz = lax.axis_size("rows") // PLANE
    chunk = (height, columns)
    dma = pltpu.SemaphoreType.DMA
    out = pl.pallas_call(
        functools.partial(reduce_body, nz, ny),
        out_shape=jax.ShapeDtypeStruct((PLANE,) + chunk, jnp.float32),
        in_specs=[VMEM],
        out_specs=VMEM,
        scratch_shapes=[
            pltpu.VMEM((PLANE,) + chunk, jnp.float32),
            pltpu.VMEM((ny,) + chunk, jnp.float32),
            pltpu.VMEM((nz,) + chunk, jnp.float32),
            pltpu.VMEM((3,) + chunk, jnp.float32),
            dma((PLANE,)),
            dma((PLANE,)),
            dma((ny,)),
            dma((ny,)),
            dma((nz,)),
            dma((nz,)),
            dma((PLANE,)),
            dma((PLANE,)),
        ],
        compiler_params=pltpu.CompilerParams(collective_id=0, has_side_effects=True),
        name="gram_reduce",
    )(gram.reshape((PLANE,) + chunk))
    return out.reshape(columns, columns)


def lower_inverse_of(gram, total_rows):
    lower = jnp.linalg.cholesky(total_gram(gram) / total_rows)
    identity = jnp.eye(gram.shape[0], dtype=jnp.float32)
    return lax.linalg.triangular_solve(lower, identity, left_side=True, lower=True)


def exchange_tiles(tiles, requested, owner):
    sent = jnp.take(tiles, requested, axis=0, mode="clip")
    got = lax.all_to_all(sent, "rows", split_axis=0, concat_axis=0, tiled=True)
    return jnp.take(got, owner, axis=0, mode="clip")


def shards(features, length_scale, prior, partners, counts, projection):
    tiles, slots = partners.shape[1:]
    size = features.shape[1] // tiles
    columns = projection.shape[1]
    nrows = lax.axis_size("rows")
    device_index = lax.axis_index("rows")
    own_rows = features[0].reshape(tiles, size, features.shape[2])
    own_side = jnp.stack(
        [length_scale[0].reshape(tiles, size), prior[0].reshape(tiles, size)], axis=1
    )
    lists = partners[0]
    far_tiles = lists[:, NEAR:].reshape(-1)
    owner = far_tiles // tiles
    hits = owner[:, None] == jnp.arange(nrows, dtype=jnp.int32)[None, :]
    wanted = jnp.sum(jnp.where(hits, (far_tiles % tiles)[:, None], 0), axis=0)
    requested = lax.all_to_all(wanted, "rows", split_axis=0, concat_axis=0, tiled=True)
    table = (lists - device_index * tiles).reshape(-1)

    far_side = exchange_tiles(own_side, requested, owner)
    far_rows = exchange_tiles(own_rows, requested, owner)
    pool = jnp.concatenate([own_rows, far_rows], axis=0)
    side = jnp.concatenate([own_side, far_side], axis=0).astype(jnp.float32)
    band = side[:, 0:1, :]
    prior_rows = side[:, 1:2, :]
    kernel_half, own_inverse = build_kernel(table, counts[0], pool, band, tiles, slots)
    far_inverse = exchange_tiles(own_inverse.astype(jnp.bfloat16), requested, owner)
    inverse = jnp.concatenate([own_inverse, far_inverse.astype(jnp.float32)], axis=0)
    raw, degree, gram = first_walk(
        table, pool, prior_rows, inverse, projection.T, kernel_half
    )
    total_rows = nrows * lax.axis_size("grp") * tiles * size
    basis, own_next = first_basis_of(lower_inverse_of(gram, total_rows), raw, own_inverse)
    far_next = exchange_tiles(own_next, requested, owner)
    second_raw, second_gram = second_walk(table, own_next, far_next, degree, kernel_half)
    embedding = jnp.dot(
        lower_inverse_of(second_gram, total_rows), second_raw, precision=lax.Precision.HIGHEST
    )
    return basis[None], embedding[None]


def solution(mesh):
    in_specs = (
        P("grp", "rows", None),
        P("grp", "rows"),
        P("grp", "rows"),
        P("grp", "rows", None),
        P("grp", "rows"),
        P(),
    )
    out_specs = (P("grp", None, "rows"), P("grp", None, "rows"))
    return jax.shard_map(shards, mesh=mesh, in_specs=in_specs, out_specs=out_specs, check_vma=False)
```

```python
import functools

import jax
import jax.numpy as jnp
from jax import lax
from jax.experimental import pallas as pl
from jax.experimental.pallas import tpu as pltpu
from jax.sharding import PartitionSpec as P

NEAR = 13
PLANE = 8
MESH = pl.DeviceIdType.MESH
VMEM = pl.BlockSpec(memory_space=pltpu.VMEM)
SMEM = pl.BlockSpec(memory_space=pltpu.SMEM)


def nt_dot(left, right, precision=None):
    return lax.dot_general(
        left,
        right,
        (((1,), (1,)), ((), ())),
        precision=precision,
        preferred_element_type=jnp.float32,
    )


def load_norm(rows):
    wide = rows.astype(jnp.float32)
    norm = jnp.sum(wide * wide, axis=1, keepdims=True)
    return jnp.broadcast_to(-norm, (rows.shape[0], rows.shape[0]))


def column_band(row):
    return jnp.transpose(jnp.broadcast_to(row, (row.shape[1], row.shape[1])))


def kernel_value(rows, norm, band, doubled, own_norm, own_band):
    level = jnp.minimum(nt_dot(rows, doubled) + (norm + own_norm), 0.0)
    return jnp.exp(level / (band + own_band))


def fold_rows(value):
    return jnp.sum(value.reshape(value.shape[0] // 8, 8, value.shape[1]), axis=0)


def near_kernel_body(
    tiles, slots, table, counts, pool, band, kernel_half, density, norm_a, norm_b, band_b
):
    size = pool.shape[1]

    def prepare(index, carry):
        wide = load_norm(pool[index])
        norm_b[index] = wide
        band_b[index] = column_band(band[index])
        norm_a[index] = jnp.transpose(wide)[0:1, :]
        return carry

    lax.fori_loop(0, tiles, prepare, 0)

    def one_tile(tile, carry):
        doubled = pool[tile] * jnp.bfloat16(2)
        own_norm = norm_a[tile]
        own_band = band[tile]
        live = counts[tile]
        total = jnp.zeros((8, size), jnp.float32)
        for slot in range(NEAR):
            index = table[tile * slots + slot]
            value = kernel_value(
                pool[index], norm_b[index], band_b[index], doubled, own_norm, own_band
            )
            if slot == NEAR - 1:
                value = jnp.where(slot < live, value, 0.0)
            kernel_half[tile, slot] = value.astype(jnp.bfloat16)
            total = total + fold_rows(value)
        density[tile] = jnp.sum(total, axis=0, keepdims=True)
        return carry

    lax.fori_loop(0, tiles, one_tile, 0)


def near_kernel(table, counts, pool, band, slots):
    tiles, size, _ = pool.shape
    return pl.pallas_call(
        functools.partial(near_kernel_body, tiles, slots),
        out_shape=(
            jax.ShapeDtypeStruct((tiles, NEAR, size, size), jnp.bfloat16),
            jax.ShapeDtypeStruct((tiles, 1, size), jnp.float32),
            jax.ShapeDtypeStruct((tiles, 1, size), jnp.float32),
        ),
        in_specs=[SMEM, SMEM, VMEM, VMEM],
        out_specs=(VMEM, VMEM, VMEM),
        scratch_shapes=[pltpu.VMEM((tiles, size, size), jnp.float32)] * 2,
        cost_estimate=cost(tiles * NEAR * size * size, 400),
        name="near_kernel",
    )(table, counts, pool, band)


def far_kernel_body(tiles, slots, counts, pool, band, far, far_band, norm_a, near, kernel_half, inverse):
    far_slots = slots - NEAR

    def one_tile(tile, carry):
        doubled = pool[tile] * jnp.bfloat16(2)
        live = counts[tile]
        total = jnp.zeros((8, pool.shape[1]), jnp.float32)
        for slot in range(far_slots):
            index = tile * far_slots + slot
            rows = far[index]
            value = kernel_value(
                rows,
                load_norm(rows),
                column_band(far_band[index]),
                doubled,
                norm_a[tile],
                band[tile],
            )
            value = jnp.where(slot + NEAR < live, value, 0.0)
            kernel_half[tile, slot] = value.astype(jnp.bfloat16)
            total = total + fold_rows(value)
        inverse[tile] = 1.0 / (near[tile] + jnp.sum(total, axis=0, keepdims=True))
        return carry

    lax.fori_loop(0, tiles, one_tile, 0, unroll=2)


def far_kernel(counts, pool, band, far, far_band, norm_a, near, slots):
    tiles, size, _ = pool.shape
    return pl.pallas_call(
        functools.partial(far_kernel_body, tiles, slots),
        out_shape=(
            jax.ShapeDtypeStruct((tiles, slots - NEAR, size, size), jnp.bfloat16),
            jax.ShapeDtypeStruct((tiles, 1, size), jnp.float32),
        ),
        in_specs=[SMEM] + [VMEM] * 6,
        out_specs=(VMEM, VMEM),
        name="far_kernel",
    )(counts, pool, band, far, far_band, norm_a, near)


def cost(flops, scale):
    return pl.CostEstimate(flops=flops * scale, bytes_accessed=flops * 4, transcendentals=flops)


def scale_start(projection, rows, prior, inv):
    start = nt_dot(projection, rows)
    scaled = (start * (prior * inv)).astype(jnp.bfloat16)
    high = inv.astype(jnp.bfloat16).astype(jnp.float32)
    row = lax.broadcasted_iota(jnp.int32, (16, inv.shape[1]), 0)
    extra = jnp.where(row == 0, high, jnp.where(row == 1, inv - high, 0.0))
    return scaled, extra.astype(jnp.bfloat16)


def near_walk_body(
    tiles, slots, table, pool, prior, inverse, projection, kernel_half, partial, scaled
):
    columns = projection.shape[0]

    def prepare(index, carry):
        main, extra = scale_start(projection[...], pool[index], prior[index], inverse[index])
        scaled[index, 0:columns, :] = main
        scaled[index, columns : columns + 16, :] = extra
        return carry

    lax.fori_loop(0, tiles, prepare, 0, unroll=2)

    def one_tile(tile, carry):
        total = jnp.zeros(partial.shape[1:], jnp.float32)
        for slot in range(NEAR):
            total = total + jnp.dot(
                scaled[table[tile * slots + slot]],
                kernel_half[tile, slot],
                preferred_element_type=jnp.float32,
            )
        partial[tile] = total
        return carry

    lax.fori_loop(0, tiles, one_tile, 0)


def near_walk(table, pool, prior, inverse, projection, kernel_half, slots):
    tiles, _, size, _ = kernel_half.shape
    height = projection.shape[0] + 16
    return pl.pallas_call(
        functools.partial(near_walk_body, tiles, slots),
        out_shape=jax.ShapeDtypeStruct((tiles, height, size), jnp.float32),
        in_specs=[SMEM] + [VMEM] * 5,
        out_specs=VMEM,
        scratch_shapes=[pltpu.VMEM((tiles, height, size), jnp.bfloat16)],
        cost_estimate=cost(tiles * NEAR * size * size, 160),
        name="near_walk",
    )(table, pool, prior, inverse, projection, kernel_half)


def far_walk_body(
    tiles, far, prior, inverse, projection, kernel_half, partial, raw, half, degree, gram, scaled
):
    size = far.shape[1]
    columns = projection.shape[0]
    far_slots = kernel_half.shape[1]
    gram[...] = jnp.zeros_like(gram)

    def prepare(index, carry):
        main, extra = scale_start(projection[...], far[index], prior[index], inverse[index])
        scaled[index, 0:columns, :] = main
        scaled[index, columns : columns + 16, :] = extra
        return carry

    lax.fori_loop(0, far.shape[0], prepare, 0, unroll=4)

    def one_tile(tile, carry):
        total = partial[tile]
        for slot in range(far_slots):
            total = total + jnp.dot(
                scaled[tile * far_slots + slot],
                kernel_half[tile, slot],
                preferred_element_type=jnp.float32,
            )
        below = total[columns : columns + 1] + total[columns + 1 : columns + 2]
        degree[tile] = below
        value = total[0:columns] / below
        raw[:, pl.ds(pl.multiple_of(tile * size, size), size)] = value
        half[tile] = value.astype(jnp.bfloat16)
        return carry

    lax.fori_loop(0, tiles, one_tile, 0, unroll=2)
    gram[...] = nt_dot(raw[...], raw[...], lax.Precision.HIGHEST)


def far_walk(far, prior, inverse, projection, kernel_half, partial):
    tiles, _, size, _ = kernel_half.shape
    columns = projection.shape[0]
    return pl.pallas_call(
        functools.partial(far_walk_body, tiles),
        out_shape=(
            jax.ShapeDtypeStruct((columns, tiles * size), jnp.float32),
            jax.ShapeDtypeStruct((tiles, columns, size), jnp.bfloat16),
            jax.ShapeDtypeStruct((tiles, 1, size), jnp.float32),
            jax.ShapeDtypeStruct((columns, columns), jnp.float32),
        ),
        in_specs=[VMEM] * 6,
        out_specs=(VMEM,) * 4,
        scratch_shapes=[pltpu.VMEM((far.shape[0], columns + 16, size), jnp.bfloat16)],
        name="far_walk",
    )(far, prior, inverse, projection, kernel_half, partial)


def near_apply_body(
    tiles, slots, table, lower_inverse, raw, inverse, kernel_half, basis, partial, scaled
):
    size = inverse.shape[2]
    value = jnp.dot(
        lower_inverse[...],
        raw[...],
        precision=lax.Precision.HIGHEST,
        preferred_element_type=jnp.float32,
    )
    basis[...] = value
    for tile in range(tiles):
        part = value[:, tile * size : (tile + 1) * size]
        scaled[tile] = (part * inverse[tile]).astype(jnp.bfloat16)

    def one_tile(tile, carry):
        total = jnp.zeros(partial.shape[1:], jnp.float32)
        for slot in range(NEAR):
            total = total + jnp.dot(
                scaled[table[tile * slots + slot]],
                kernel_half[tile, slot],
                preferred_element_type=jnp.float32,
            )
        partial[tile] = total
        return carry

    lax.fori_loop(0, tiles, one_tile, 0)


def near_apply(table, lower_inverse, raw, inverse, kernel_half, slots):
    tiles, _, size, _ = kernel_half.shape
    columns = raw.shape[0]
    return pl.pallas_call(
        functools.partial(near_apply_body, tiles, slots),
        out_shape=(
            jax.ShapeDtypeStruct(raw.shape, jnp.float32),
            jax.ShapeDtypeStruct((tiles, columns, size), jnp.float32),
        ),
        in_specs=[SMEM] + [VMEM] * 4,
        out_specs=(VMEM, VMEM),
        scratch_shapes=[pltpu.VMEM((tiles, columns, size), jnp.bfloat16)],
        cost_estimate=cost(tiles * NEAR * size * size, 128),
        name="near_apply",
    )(table, lower_inverse, raw, inverse, kernel_half)


def far_apply_body(tiles, lower_inverse, far, inverse, degree, kernel_half, partial, raw, gram, scaled):
    size = far.shape[2]
    far_slots = kernel_half.shape[1]

    def prepare(index, carry):
        basis = jnp.dot(
            lower_inverse[...],
            far[index].astype(jnp.float32),
            precision=lax.Precision.HIGHEST,
            preferred_element_type=jnp.float32,
        )
        scaled[index] = (basis * inverse[index]).astype(jnp.bfloat16)
        return carry

    lax.fori_loop(0, far.shape[0], prepare, 0, unroll=4)

    def one_tile(tile, carry):
        total = partial[tile]
        for slot in range(far_slots):
            total = total + jnp.dot(
                scaled[tile * far_slots + slot],
                kernel_half[tile, slot],
                preferred_element_type=jnp.float32,
            )
        raw[:, pl.ds(pl.multiple_of(tile * size, size), size)] = total / degree[tile]
        return carry

    lax.fori_loop(0, tiles, one_tile, 0, unroll=2)
    gram[...] = nt_dot(raw[...], raw[...], lax.Precision.HIGHEST)


def far_apply(lower_inverse, far, inverse, degree, kernel_half, partial):
    tiles, columns, size = partial.shape
    return pl.pallas_call(
        functools.partial(far_apply_body, tiles),
        out_shape=(
            jax.ShapeDtypeStruct((columns, tiles * size), jnp.float32),
            jax.ShapeDtypeStruct((columns, columns), jnp.float32),
        ),
        in_specs=[VMEM] * 6,
        out_specs=(VMEM, VMEM),
        scratch_shapes=[pltpu.VMEM(far.shape, jnp.bfloat16)],
        name="far_apply",
    )(lower_inverse, far, inverse, degree, kernel_half, partial)


def reduce_body(nz, ny, local, out, parts_w, parts_y, parts_z, stage, sw, rw, sy, ry, sz, rz, sa, ra):
    row = lax.axis_index("rows")
    y = lax.axis_index("grp")
    w = row % PLANE
    z = row // PLANE

    def peer_w(step):
        other = (w + step) % PLANE
        return other, (z * PLANE + other, y)

    def peer_y(step):
        other = (y + step) % ny
        return other, (row, other)

    def peer_z(step):
        other = (z + step) % nz
        return other, (other * PLANE + w, y)

    barrier = pltpu.get_barrier_semaphore()
    for count, peer in ((PLANE, peer_w), (ny, peer_y), (nz, peer_z)):

        def greet(step, carry):
            pl.semaphore_signal(barrier, inc=1, device_id=peer(step)[1], device_id_type=MESH)
            return carry

        lax.fori_loop(1, count, greet, 0)
    pl.semaphore_wait(barrier, PLANE + ny + nz - 3)

    def exchange(count, peer, me, source, target, send, recv):
        def copy(step, mine):
            other, device = peer(step)
            return pltpu.make_async_remote_copy(
                src_ref=source(other),
                dst_ref=target.at[me if mine else other],
                send_sem=send.at[other],
                recv_sem=recv.at[me if mine else other],
                device_id=device,
                device_id_type=MESH,
            )

        def start(step, carry):
            copy(step, True).start()
            return carry

        def finish(step, carry):
            copy(step, True).wait_send()
            copy(step, False).wait_recv()
            return carry

        lax.fori_loop(1, count, start, 0)
        lax.fori_loop(1, count, finish, 0)

    exchange(PLANE, peer_w, w, lambda other: local.at[other], parts_w, sw, rw)
    parts_w[w] = local[w]
    stage[0] = jnp.sum(parts_w[...], axis=0)
    exchange(ny, peer_y, y, lambda other: stage.at[0], parts_y, sy, ry)
    parts_y[y] = stage[0]
    stage[1] = jnp.sum(parts_y[...], axis=0)
    exchange(nz, peer_z, z, lambda other: stage.at[1], parts_z, sz, rz)
    parts_z[z] = stage[1]
    stage[2] = jnp.sum(parts_z[...], axis=0)
    exchange(PLANE, peer_w, w, lambda other: stage.at[2], out, sa, ra)
    out[w] = stage[2]


def total_gram(gram):
    columns = gram.shape[0]
    height = columns // PLANE
    ny = lax.axis_size("grp")
    nz = lax.axis_size("rows") // PLANE
    chunk = (height, columns)
    dma = pltpu.SemaphoreType.DMA
    out = pl.pallas_call(
        functools.partial(reduce_body, nz, ny),
        out_shape=jax.ShapeDtypeStruct((PLANE,) + chunk, jnp.float32),
        in_specs=[VMEM],
        out_specs=VMEM,
        scratch_shapes=[
            pltpu.VMEM((PLANE,) + chunk, jnp.float32),
            pltpu.VMEM((ny,) + chunk, jnp.float32),
            pltpu.VMEM((nz,) + chunk, jnp.float32),
            pltpu.VMEM((3,) + chunk, jnp.float32),
            dma((PLANE,)),
            dma((PLANE,)),
            dma((ny,)),
            dma((ny,)),
            dma((nz,)),
            dma((nz,)),
            dma((PLANE,)),
            dma((PLANE,)),
        ],
        compiler_params=pltpu.CompilerParams(collective_id=0, has_side_effects=True),
        name="gram_reduce",
    )(gram.reshape((PLANE,) + chunk))
    return out.reshape(columns, columns)


def lower_inverse_of(gram, total_rows):
    lower = jnp.linalg.cholesky(total_gram(gram) / total_rows)
    identity = jnp.eye(gram.shape[0], dtype=jnp.float32)
    return lax.linalg.triangular_solve(lower, identity, left_side=True, lower=True)


def exchange_tiles(tiles, requested, owner):
    sent = jnp.take(tiles, requested, axis=0, mode="clip")
    got = lax.all_to_all(sent, "rows", split_axis=0, concat_axis=0, tiled=True)
    return jnp.take(got, owner, axis=0, mode="clip")


def shards(features, length_scale, prior, partners, counts, projection):
    tiles, slots = partners.shape[1:]
    size = features.shape[1] // tiles
    columns = projection.shape[1]
    nrows = lax.axis_size("rows")
    device_index = lax.axis_index("rows")
    own_rows = features[0].reshape(tiles, size, features.shape[2])
    own_side = jnp.stack(
        [length_scale[0].reshape(tiles, size), prior[0].reshape(tiles, size)], axis=1
    )
    lists = partners[0]
    far_tiles = lists[:, NEAR:].reshape(-1)
    owner = far_tiles // tiles
    hits = owner[:, None] == jnp.arange(nrows, dtype=jnp.int32)[None, :]
    wanted = jnp.sum(jnp.where(hits, (far_tiles % tiles)[:, None], 0), axis=0)
    requested = lax.all_to_all(wanted, "rows", split_axis=0, concat_axis=0, tiled=True)
    table = (lists - device_index * tiles).reshape(-1)

    far_side = exchange_tiles(own_side, requested, owner).astype(jnp.float32)
    far_rows = exchange_tiles(own_rows, requested, owner)
    side = own_side.astype(jnp.float32)
    own_band, own_prior = side[:, 0:1, :], side[:, 1:2, :]
    far_band, far_prior = far_side[:, 0:1, :], far_side[:, 1:2, :]
    directions = projection.T
    near_half, near_density, norms = near_kernel(table, counts[0], own_rows, own_band, slots)
    far_half, own_inverse = far_kernel(
        counts[0], own_rows, own_band, far_rows, far_band, norms, near_density, slots
    )
    far_inverse = exchange_tiles(own_inverse.astype(jnp.bfloat16), requested, owner)
    far_inverse = far_inverse.astype(jnp.float32)
    near_part = near_walk(table, own_rows, own_prior, own_inverse, directions, near_half, slots)
    raw, raw_half, degree, gram = far_walk(
        far_rows, far_prior, far_inverse, directions, far_half, near_part
    )
    far_raw = exchange_tiles(raw_half, requested, owner)
    total_rows = nrows * lax.axis_size("grp") * tiles * size
    lower_inverse = lower_inverse_of(gram, total_rows)
    basis, near_second = near_apply(table, lower_inverse, raw, own_inverse, near_half, slots)
    second_raw, second_gram = far_apply(
        lower_inverse, far_raw, far_inverse, degree, far_half, near_second
    )
    embedding = jnp.dot(
        lower_inverse_of(second_gram, total_rows), second_raw, precision=lax.Precision.HIGHEST
    )
    return basis[None], embedding[None]


def solution(mesh):
    in_specs = (
        P("grp", "rows", None),
        P("grp", "rows"),
        P("grp", "rows"),
        P("grp", "rows", None),
        P("grp", "rows"),
        P(),
    )
    out_specs = (P("grp", None, "rows"), P("grp", None, "rows"))
    return jax.shard_map(shards, mesh=mesh, in_specs=in_specs, out_specs=out_specs, check_vma=False)
```

```python
import functools

import jax
import jax.numpy as jnp
from jax import lax
from jax.experimental import pallas as pl
from jax.experimental.pallas import tpu as pltpu
from jax.sharding import PartitionSpec as P

NEAR = 13
PLANE = 8
MESH = pl.DeviceIdType.MESH
VMEM = pl.BlockSpec(memory_space=pltpu.VMEM)
SMEM = pl.BlockSpec(memory_space=pltpu.SMEM)


def nt_dot(left, right, precision=None):
    return lax.dot_general(
        left,
        right,
        (((1,), (1,)), ((), ())),
        precision=precision,
        preferred_element_type=jnp.float32,
    )


def load_norm(rows):
    wide = rows.astype(jnp.float32)
    norm = jnp.sum(wide * wide, axis=1, keepdims=True)
    return jnp.broadcast_to(-norm, (rows.shape[0], rows.shape[0]))


def column_band(row):
    return jnp.transpose(jnp.broadcast_to(row, (row.shape[1], row.shape[1])))


def kernel_value(rows, norm, band, doubled, own_norm, own_band):
    level = jnp.minimum(nt_dot(rows, doubled) + (norm + own_norm), 0.0)
    return jnp.exp(level / (band + own_band))


def fold_rows(value):
    return jnp.sum(value.reshape(value.shape[0] // 8, 8, value.shape[1]), axis=0)


def near_kernel_body(
    tiles, slots, table, counts, pool, band, kernel_half, density, norm_a, norm_b, band_b
):
    size = pool.shape[1]

    def prepare(index, carry):
        wide = load_norm(pool[index])
        norm_b[index] = wide
        band_b[index] = column_band(band[index])
        norm_a[index] = jnp.transpose(wide)[0:1, :]
        return carry

    lax.fori_loop(0, tiles, prepare, 0)

    def one_tile(tile, carry):
        doubled = pool[tile] * jnp.bfloat16(2)
        own_norm = norm_a[tile]
        own_band = band[tile]
        live = counts[tile]
        total = jnp.zeros((8, size), jnp.float32)
        for slot in range(NEAR):
            index = table[tile * slots + slot]
            value = kernel_value(
                pool[index], norm_b[index], band_b[index], doubled, own_norm, own_band
            )
            if slot == NEAR - 1:
                value = jnp.where(slot < live, value, 0.0)
            kernel_half[tile, slot] = value.astype(jnp.bfloat16)
            total = total + fold_rows(value)
        density[tile] = jnp.sum(total, axis=0, keepdims=True)
        return carry

    lax.fori_loop(0, tiles, one_tile, 0)


def near_kernel(table, counts, pool, band, slots):
    tiles, size, _ = pool.shape
    return pl.pallas_call(
        functools.partial(near_kernel_body, tiles, slots),
        out_shape=(
            jax.ShapeDtypeStruct((tiles, NEAR, size, size), jnp.bfloat16),
            jax.ShapeDtypeStruct((tiles, 1, size), jnp.float32),
            jax.ShapeDtypeStruct((tiles, 1, size), jnp.float32),
        ),
        in_specs=[SMEM, SMEM, VMEM, VMEM],
        out_specs=(VMEM, VMEM, VMEM),
        scratch_shapes=[pltpu.VMEM((tiles, size, size), jnp.float32)] * 2,
        cost_estimate=cost(tiles * NEAR * size * size, 400),
        name="near_kernel",
    )(table, counts, pool, band)


def far_kernel_body(tiles, slots, counts, pool, band, far, far_band, norm_a, near, kernel_half, inverse):
    far_slots = slots - NEAR

    def one_tile(tile, carry):
        doubled = pool[tile] * jnp.bfloat16(2)
        live = counts[tile]
        total = jnp.zeros((8, pool.shape[1]), jnp.float32)
        for slot in range(far_slots):
            index = tile * far_slots + slot
            rows = far[index]
            value = kernel_value(
                rows,
                load_norm(rows),
                column_band(far_band[index]),
                doubled,
                norm_a[tile],
                band[tile],
            )
            value = jnp.where(slot + NEAR < live, value, 0.0)
            kernel_half[tile, slot] = value.astype(jnp.bfloat16)
            total = total + fold_rows(value)
        inverse[tile] = 1.0 / (near[tile] + jnp.sum(total, axis=0, keepdims=True))
        return carry

    lax.fori_loop(0, tiles, one_tile, 0, unroll=2)


def far_kernel(counts, pool, band, far, far_band, norm_a, near, slots):
    tiles, size, _ = pool.shape
    return pl.pallas_call(
        functools.partial(far_kernel_body, tiles, slots),
        out_shape=(
            jax.ShapeDtypeStruct((tiles, slots - NEAR, size, size), jnp.bfloat16),
            jax.ShapeDtypeStruct((tiles, 1, size), jnp.float32),
        ),
        in_specs=[SMEM] + [VMEM] * 6,
        out_specs=(VMEM, VMEM),
        name="far_kernel",
    )(counts, pool, band, far, far_band, norm_a, near)


def cost(flops, scale):
    return pl.CostEstimate(flops=flops * scale, bytes_accessed=flops * 4, transcendentals=flops)


def scale_start(projection, rows, prior, inv):
    start = nt_dot(projection, rows)
    scaled = (start * (prior * inv)).astype(jnp.bfloat16)
    high = inv.astype(jnp.bfloat16).astype(jnp.float32)
    row = lax.broadcasted_iota(jnp.int32, (16, inv.shape[1]), 0)
    extra = jnp.where(row == 0, high, jnp.where(row == 1, inv - high, 0.0))
    return scaled, extra.astype(jnp.bfloat16)


def near_walk_body(
    tiles, slots, table, pool, prior, inverse, projection, kernel_half, partial, scaled
):
    columns = projection.shape[0]

    def prepare(index, carry):
        main, extra = scale_start(projection[...], pool[index], prior[index], inverse[index])
        scaled[index, 0:columns, :] = main
        scaled[index, columns : columns + 16, :] = extra
        return carry

    lax.fori_loop(0, tiles, prepare, 0, unroll=2)

    def one_tile(tile, carry):
        total = jnp.zeros(partial.shape[1:], jnp.float32)
        for slot in range(NEAR):
            total = total + jnp.dot(
                scaled[table[tile * slots + slot]],
                kernel_half[tile, slot],
                preferred_element_type=jnp.float32,
            )
        partial[tile] = total
        return carry

    lax.fori_loop(0, tiles, one_tile, 0)


def near_walk(table, pool, prior, inverse, projection, kernel_half, slots):
    tiles, _, size, _ = kernel_half.shape
    height = projection.shape[0] + 16
    return pl.pallas_call(
        functools.partial(near_walk_body, tiles, slots),
        out_shape=jax.ShapeDtypeStruct((tiles, height, size), jnp.float32),
        in_specs=[SMEM] + [VMEM] * 5,
        out_specs=VMEM,
        scratch_shapes=[pltpu.VMEM((tiles, height, size), jnp.bfloat16)],
        cost_estimate=cost(tiles * NEAR * size * size, 160),
        name="near_walk",
    )(table, pool, prior, inverse, projection, kernel_half)


def far_walk_body(
    tiles, far, prior, inverse, projection, kernel_half, partial, raw, half, degree, gram, scaled
):
    size = far.shape[1]
    columns = projection.shape[0]
    far_slots = kernel_half.shape[1]
    gram[...] = jnp.zeros_like(gram)

    def prepare(index, carry):
        main, extra = scale_start(projection[...], far[index], prior[index], inverse[index])
        scaled[index, 0:columns, :] = main
        scaled[index, columns : columns + 16, :] = extra
        return carry

    lax.fori_loop(0, far.shape[0], prepare, 0, unroll=4)

    def one_tile(tile, carry):
        total = partial[tile]
        for slot in range(far_slots):
            total = total + jnp.dot(
                scaled[tile * far_slots + slot],
                kernel_half[tile, slot],
                preferred_element_type=jnp.float32,
            )
        below = total[columns : columns + 1] + total[columns + 1 : columns + 2]
        degree[tile] = below
        value = total[0:columns] / below
        raw[:, pl.ds(pl.multiple_of(tile * size, size), size)] = value
        half[tile] = value.astype(jnp.bfloat16)
        return carry

    lax.fori_loop(0, tiles, one_tile, 0, unroll=2)
    gram[...] = nt_dot(raw[...], raw[...], lax.Precision.HIGHEST)


def far_walk(far, prior, inverse, projection, kernel_half, partial):
    tiles, _, size, _ = kernel_half.shape
    columns = projection.shape[0]
    return pl.pallas_call(
        functools.partial(far_walk_body, tiles),
        out_shape=(
            jax.ShapeDtypeStruct((columns, tiles * size), jnp.float32),
            jax.ShapeDtypeStruct((tiles, columns, size), jnp.bfloat16),
            jax.ShapeDtypeStruct((tiles, 1, size), jnp.float32),
            jax.ShapeDtypeStruct((columns, columns), jnp.float32),
        ),
        in_specs=[VMEM] * 6,
        out_specs=(VMEM,) * 4,
        scratch_shapes=[pltpu.VMEM((far.shape[0], columns + 16, size), jnp.bfloat16)],
        name="far_walk",
    )(far, prior, inverse, projection, kernel_half, partial)


def near_apply_body(
    tiles, slots, table, lower_inverse, raw, inverse, kernel_half, basis, partial, scaled
):
    size = inverse.shape[2]
    value = jnp.dot(
        lower_inverse[...],
        raw[...],
        precision=lax.Precision.HIGHEST,
        preferred_element_type=jnp.float32,
    )
    basis[...] = value
    for tile in range(tiles):
        part = value[:, tile * size : (tile + 1) * size]
        scaled[tile] = (part * inverse[tile]).astype(jnp.bfloat16)

    def one_tile(tile, carry):
        total = jnp.zeros(partial.shape[1:], jnp.float32)
        for slot in range(NEAR):
            total = total + jnp.dot(
                scaled[table[tile * slots + slot]],
                kernel_half[tile, slot],
                preferred_element_type=jnp.float32,
            )
        partial[tile] = total
        return carry

    lax.fori_loop(0, tiles, one_tile, 0)


def near_apply(table, lower_inverse, raw, inverse, kernel_half, slots):
    tiles, _, size, _ = kernel_half.shape
    columns = raw.shape[0]
    return pl.pallas_call(
        functools.partial(near_apply_body, tiles, slots),
        out_shape=(
            jax.ShapeDtypeStruct(raw.shape, jnp.float32),
            jax.ShapeDtypeStruct((tiles, columns, size), jnp.float32),
        ),
        in_specs=[SMEM] + [VMEM] * 4,
        out_specs=(VMEM, VMEM),
        scratch_shapes=[pltpu.VMEM((tiles, columns, size), jnp.bfloat16)],
        cost_estimate=cost(tiles * NEAR * size * size, 128),
        name="near_apply",
    )(table, lower_inverse, raw, inverse, kernel_half)


def far_apply_body(tiles, lower_inverse, far, inverse, degree, kernel_half, partial, raw, gram, scaled):
    size = far.shape[2]
    far_slots = kernel_half.shape[1]

    def prepare(index, carry):
        basis = jnp.dot(
            lower_inverse[...],
            far[index].astype(jnp.float32),
            precision=lax.Precision.HIGHEST,
            preferred_element_type=jnp.float32,
        )
        scaled[index] = (basis * inverse[index]).astype(jnp.bfloat16)
        return carry

    lax.fori_loop(0, far.shape[0], prepare, 0, unroll=4)

    def one_tile(tile, carry):
        total = partial[tile]
        for slot in range(far_slots):
            total = total + jnp.dot(
                scaled[tile * far_slots + slot],
                kernel_half[tile, slot],
                preferred_element_type=jnp.float32,
            )
        raw[:, pl.ds(pl.multiple_of(tile * size, size), size)] = total / degree[tile]
        return carry

    lax.fori_loop(0, tiles, one_tile, 0, unroll=2)
    gram[...] = nt_dot(raw[...], raw[...], lax.Precision.HIGHEST)


def far_apply(lower_inverse, far, inverse, degree, kernel_half, partial):
    tiles, columns, size = partial.shape
    return pl.pallas_call(
        functools.partial(far_apply_body, tiles),
        out_shape=(
            jax.ShapeDtypeStruct((columns, tiles * size), jnp.float32),
            jax.ShapeDtypeStruct((columns, columns), jnp.float32),
        ),
        in_specs=[VMEM] * 6,
        out_specs=(VMEM, VMEM),
        scratch_shapes=[pltpu.VMEM(far.shape, jnp.bfloat16)],
        name="far_apply",
    )(lower_inverse, far, inverse, degree, kernel_half, partial)


def reduce_body(nz, ny, local, out, parts_w, parts_y, parts_z, stage, sw, rw, sy, ry, sz, rz, sa, ra):
    row = lax.axis_index("rows")
    y = lax.axis_index("grp")
    w = row % PLANE
    z = row // PLANE

    def peer_w(step):
        other = (w + step) % PLANE
        return other, (z * PLANE + other, y)

    def peer_y(step):
        other = (y + step) % ny
        return other, (row, other)

    def peer_z(step):
        other = (z + step) % nz
        return other, (other * PLANE + w, y)

    barrier = pltpu.get_barrier_semaphore()
    for count, peer in ((PLANE, peer_w), (ny, peer_y), (nz, peer_z)):

        def greet(step, carry):
            pl.semaphore_signal(barrier, inc=1, device_id=peer(step)[1], device_id_type=MESH)
            return carry

        lax.fori_loop(1, count, greet, 0)
    pl.semaphore_wait(barrier, PLANE + ny + nz - 3)

    def exchange(count, peer, me, source, target, send, recv):
        def copy(step, mine):
            other, device = peer(step)
            return pltpu.make_async_remote_copy(
                src_ref=source(other),
                dst_ref=target.at[me if mine else other],
                send_sem=send.at[other],
                recv_sem=recv.at[me if mine else other],
                device_id=device,
                device_id_type=MESH,
            )

        def start(step, carry):
            copy(step, True).start()
            return carry

        def finish(step, carry):
            copy(step, True).wait_send()
            copy(step, False).wait_recv()
            return carry

        lax.fori_loop(1, count, start, 0)
        lax.fori_loop(1, count, finish, 0)

    exchange(PLANE, peer_w, w, lambda other: local.at[other], parts_w, sw, rw)
    parts_w[w] = local[w]
    stage[0] = jnp.sum(parts_w[...], axis=0)
    exchange(ny, peer_y, y, lambda other: stage.at[0], parts_y, sy, ry)
    parts_y[y] = stage[0]
    stage[1] = jnp.sum(parts_y[...], axis=0)
    exchange(nz, peer_z, z, lambda other: stage.at[1], parts_z, sz, rz)
    parts_z[z] = stage[1]
    stage[2] = jnp.sum(parts_z[...], axis=0)
    exchange(PLANE, peer_w, w, lambda other: stage.at[2], out, sa, ra)
    out[w] = stage[2]


def swap_body(count, sent, got, send, recv):
    me = lax.axis_index("rows")
    y = lax.axis_index("grp")

    def other_of(step):
        return (me + step) % count

    barrier = pltpu.get_barrier_semaphore()

    def greet(step, carry):
        pl.semaphore_signal(barrier, inc=1, device_id=(other_of(step), y), device_id_type=MESH)
        return carry

    lax.fori_loop(1, count, greet, 0)
    pl.semaphore_wait(barrier, count - 1)

    def copy(step, mine):
        other = other_of(step)
        slot = me if mine else other
        return pltpu.make_async_remote_copy(
            src_ref=sent.at[other],
            dst_ref=got.at[slot],
            send_sem=send.at[other],
            recv_sem=recv.at[slot],
            device_id=(other, y),
            device_id_type=MESH,
        )

    def start(step, carry):
        copy(step, True).start()
        return carry

    def finish(step, carry):
        copy(step, True).wait_send()
        copy(step, False).wait_recv()
        return carry

    lax.fori_loop(1, count, start, 0)
    got[me] = sent[me]
    lax.fori_loop(1, count, finish, 0)


def swap(sent, collective_id):
    count = sent.shape[0]
    dma = pltpu.SemaphoreType.DMA
    return pl.pallas_call(
        functools.partial(swap_body, count),
        out_shape=jax.ShapeDtypeStruct(sent.shape, sent.dtype),
        in_specs=[VMEM],
        out_specs=VMEM,
        scratch_shapes=[dma((count,)), dma((count,))],
        compiler_params=pltpu.CompilerParams(collective_id=collective_id, has_side_effects=True),
        name="swap_%d" % collective_id,
    )(sent)


def total_gram(gram):
    columns = gram.shape[0]
    height = columns // PLANE
    ny = lax.axis_size("grp")
    nz = lax.axis_size("rows") // PLANE
    chunk = (height, columns)
    dma = pltpu.SemaphoreType.DMA
    out = pl.pallas_call(
        functools.partial(reduce_body, nz, ny),
        out_shape=jax.ShapeDtypeStruct((PLANE,) + chunk, jnp.float32),
        in_specs=[VMEM],
        out_specs=VMEM,
        scratch_shapes=[
            pltpu.VMEM((PLANE,) + chunk, jnp.float32),
            pltpu.VMEM((ny,) + chunk, jnp.float32),
            pltpu.VMEM((nz,) + chunk, jnp.float32),
            pltpu.VMEM((3,) + chunk, jnp.float32),
            dma((PLANE,)),
            dma((PLANE,)),
            dma((ny,)),
            dma((ny,)),
            dma((nz,)),
            dma((nz,)),
            dma((PLANE,)),
            dma((PLANE,)),
        ],
        compiler_params=pltpu.CompilerParams(collective_id=0, has_side_effects=True),
        name="gram_reduce",
    )(gram.reshape((PLANE,) + chunk))
    return out.reshape(columns, columns)


def lower_inverse_of(gram, total_rows):
    lower = jnp.linalg.cholesky(gram / total_rows)
    identity = jnp.eye(gram.shape[0], dtype=jnp.float32)
    return lax.linalg.triangular_solve(lower, identity, left_side=True, lower=True)


def exchange_tiles(tiles, requested, owner):
    sent = jnp.take(tiles, requested, axis=0, mode="clip")
    got = lax.all_to_all(sent, "rows", split_axis=0, concat_axis=0, tiled=True)
    return jnp.take(got, owner, axis=0, mode="clip")


def shards(features, length_scale, prior, partners, counts, projection):
    tiles, slots = partners.shape[1:]
    size = features.shape[1] // tiles
    columns = projection.shape[1]
    nrows = lax.axis_size("rows")
    device_index = lax.axis_index("rows")
    own_rows = features[0].reshape(tiles, size, features.shape[2])
    own_side = jnp.stack(
        [length_scale[0].reshape(tiles, size), prior[0].reshape(tiles, size)], axis=1
    )
    lists = partners[0]
    far_tiles = lists[:, NEAR:].reshape(-1)
    owner = far_tiles // tiles
    hits = owner[:, None] == jnp.arange(nrows, dtype=jnp.int32)[None, :]
    wanted = jnp.sum(jnp.where(hits, (far_tiles % tiles)[:, None], 0), axis=0)
    wide = jnp.broadcast_to(wanted[:, None, None], (nrows, 1, 128))
    requested = swap(wide, 1)[:, 0, 0]
    table = (lists - device_index * tiles).reshape(-1)

    far_rows = exchange_tiles(own_rows, requested, owner)
    side = own_side.astype(jnp.float32)
    own_band, own_prior = side[:, 0:1, :], side[:, 1:2, :]
    directions = projection.T
    near_half, near_density, norms = near_kernel(table, counts[0], own_rows, own_band, slots)
    near_density, far_side = lax.optimization_barrier(
        (near_density, jnp.take(own_side, requested, axis=0, mode="clip"))
    )
    far_side = jnp.take(swap(far_side, 2), owner, axis=0, mode="clip").astype(jnp.float32)
    far_band, far_prior = far_side[:, 0:1, :], far_side[:, 1:2, :]
    far_half, own_inverse = far_kernel(
        counts[0], own_rows, own_band, far_rows, far_band, norms, near_density, slots
    )
    far_inverse = exchange_tiles(own_inverse.astype(jnp.bfloat16), requested, owner)
    far_inverse = far_inverse.astype(jnp.float32)
    near_part = near_walk(table, own_rows, own_prior, own_inverse, directions, near_half, slots)
    raw, raw_half, degree, gram = far_walk(
        far_rows, far_prior, far_inverse, directions, far_half, near_part
    )
    middle = columns // 2
    low_raw = exchange_tiles(raw_half[:, :middle], requested, owner)
    gram, late_half = lax.optimization_barrier((total_gram(gram), raw_half[:, middle:]))
    high_raw = exchange_tiles(late_half, requested, owner)
    far_raw = jnp.concatenate([low_raw, high_raw], axis=1)
    total_rows = nrows * lax.axis_size("grp") * tiles * size
    lower_inverse = lower_inverse_of(gram, total_rows)
    basis, near_second = near_apply(table, lower_inverse, raw, own_inverse, near_half, slots)
    second_raw, second_gram = far_apply(
        lower_inverse, far_raw, far_inverse, degree, far_half, near_second
    )
    embedding = jnp.dot(
        lower_inverse_of(total_gram(second_gram), total_rows),
        second_raw,
        precision=lax.Precision.HIGHEST,
    )
    return basis[None], embedding[None]


def solution(mesh):
    in_specs = (
        P("grp", "rows", None),
        P("grp", "rows"),
        P("grp", "rows"),
        P("grp", "rows", None),
        P("grp", "rows"),
        P(),
    )
    out_specs = (P("grp", None, "rows"), P("grp", None, "rows"))
    return jax.shard_map(shards, mesh=mesh, in_specs=in_specs, out_specs=out_specs, check_vma=False)
```

```python
import functools

import jax
import jax.numpy as jnp
from jax import lax
from jax.experimental import pallas as pl
from jax.experimental.pallas import tpu as pltpu
from jax.sharding import PartitionSpec as P

NEAR = 13
PLANE = 8
MESH = pl.DeviceIdType.MESH
VMEM = pl.BlockSpec(memory_space=pltpu.VMEM)
SMEM = pl.BlockSpec(memory_space=pltpu.SMEM)


def nt_dot(left, right, precision=None):
    return lax.dot_general(
        left,
        right,
        (((1,), (1,)), ((), ())),
        precision=precision,
        preferred_element_type=jnp.float32,
    )


def load_norm(rows):
    wide = rows.astype(jnp.float32)
    norm = jnp.sum(wide * wide, axis=1, keepdims=True)
    return jnp.broadcast_to(-norm, (rows.shape[0], rows.shape[0]))


def column_band(row):
    return jnp.transpose(jnp.broadcast_to(row, (row.shape[1], row.shape[1])))


def kernel_value(rows, norm, band, doubled, own_norm, own_band):
    level = jnp.minimum(nt_dot(rows, doubled) + (norm + own_norm), 0.0)
    return jnp.exp(level / (band + own_band))


def fold_rows(value):
    return jnp.sum(value.reshape(value.shape[0] // 8, 8, value.shape[1]), axis=0)


def near_kernel_body(
    tiles, slots, table, counts, pool, band, kernel_half, density, norm_a, norm_b, band_b
):
    size = pool.shape[1]

    def prepare(index, carry):
        wide = load_norm(pool[index])
        norm_b[index] = wide
        band_b[index] = column_band(band[index])
        norm_a[index] = jnp.transpose(wide)[0:1, :]
        return carry

    lax.fori_loop(0, tiles, prepare, 0)

    def one_tile(tile, carry):
        doubled = pool[tile] * jnp.bfloat16(2)
        own_norm = norm_a[tile]
        own_band = band[tile]
        live = counts[tile]
        total = jnp.zeros((8, size), jnp.float32)
        for slot in range(NEAR):
            index = table[tile * slots + slot]
            value = kernel_value(
                pool[index], norm_b[index], band_b[index], doubled, own_norm, own_band
            )
            if slot == NEAR - 1:
                value = jnp.where(slot < live, value, 0.0)
            kernel_half[tile, slot] = value.astype(jnp.bfloat16)
            total = total + fold_rows(value)
        density[tile] = jnp.sum(total, axis=0, keepdims=True)
        return carry

    lax.fori_loop(0, tiles, one_tile, 0)


def near_kernel(table, counts, pool, band, slots):
    tiles, size, _ = pool.shape
    return pl.pallas_call(
        functools.partial(near_kernel_body, tiles, slots),
        out_shape=(
            jax.ShapeDtypeStruct((tiles, NEAR, size, size), jnp.bfloat16),
            jax.ShapeDtypeStruct((tiles, 1, size), jnp.float32),
            jax.ShapeDtypeStruct((tiles, 1, size), jnp.float32),
        ),
        in_specs=[SMEM, SMEM, VMEM, VMEM],
        out_specs=(VMEM, VMEM, VMEM),
        scratch_shapes=[pltpu.VMEM((tiles, size, size), jnp.float32)] * 2,
        cost_estimate=cost(tiles * NEAR * size * size, 400),
        name="near_kernel",
    )(table, counts, pool, band)


def far_kernel_body(tiles, slots, counts, pool, band, far, norm_a, near, kernel_half, inverse):
    far_slots = slots - NEAR
    size = pool.shape[1]

    def one_tile(tile, carry):
        doubled = pool[tile] * jnp.bfloat16(2)
        live = counts[tile]
        total = jnp.zeros((8, pool.shape[1]), jnp.float32)
        for slot in range(far_slots):
            index = tile * far_slots + slot
            rows = far[index, 0:size, :]
            value = kernel_value(
                rows,
                load_norm(rows),
                column_band(far[index, size : size + 1, :].astype(jnp.float32)),
                doubled,
                norm_a[tile],
                band[tile],
            )
            value = jnp.where(slot + NEAR < live, value, 0.0)
            kernel_half[tile, slot] = value.astype(jnp.bfloat16)
            total = total + fold_rows(value)
        inverse[tile] = 1.0 / (near[tile] + jnp.sum(total, axis=0, keepdims=True))
        return carry

    lax.fori_loop(0, tiles, one_tile, 0, unroll=2)


def far_kernel(counts, pool, band, far, norm_a, near, slots):
    tiles, size, _ = pool.shape
    return pl.pallas_call(
        functools.partial(far_kernel_body, tiles, slots),
        out_shape=(
            jax.ShapeDtypeStruct((tiles, slots - NEAR, size, size), jnp.bfloat16),
            jax.ShapeDtypeStruct((tiles, 1, size), jnp.float32),
        ),
        in_specs=[SMEM] + [VMEM] * 5,
        out_specs=(VMEM, VMEM),
        name="far_kernel",
    )(counts, pool, band, far, norm_a, near)


def cost(flops, scale):
    return pl.CostEstimate(flops=flops * scale, bytes_accessed=flops * 4, transcendentals=flops)


def scale_start(projection, rows, prior, inv):
    start = nt_dot(projection, rows)
    scaled = (start * (prior * inv)).astype(jnp.bfloat16)
    high = inv.astype(jnp.bfloat16).astype(jnp.float32)
    row = lax.broadcasted_iota(jnp.int32, (16, inv.shape[1]), 0)
    extra = jnp.where(row == 0, high, jnp.where(row == 1, inv - high, 0.0))
    return scaled, extra.astype(jnp.bfloat16)


def near_walk_body(
    tiles, slots, table, pool, prior, inverse, projection, kernel_half, partial, scaled
):
    columns = projection.shape[0]

    def prepare(index, carry):
        main, extra = scale_start(projection[...], pool[index], prior[index], inverse[index])
        scaled[index, 0:columns, :] = main
        scaled[index, columns : columns + 16, :] = extra
        return carry

    lax.fori_loop(0, tiles, prepare, 0, unroll=2)

    def one_tile(tile, carry):
        total = jnp.zeros(partial.shape[1:], jnp.float32)
        for slot in range(NEAR):
            total = total + jnp.dot(
                scaled[table[tile * slots + slot]],
                kernel_half[tile, slot],
                preferred_element_type=jnp.float32,
            )
        partial[tile] = total
        return carry

    lax.fori_loop(0, tiles, one_tile, 0)


def near_walk(table, pool, prior, inverse, projection, kernel_half, slots):
    tiles, _, size, _ = kernel_half.shape
    height = projection.shape[0] + 16
    return pl.pallas_call(
        functools.partial(near_walk_body, tiles, slots),
        out_shape=jax.ShapeDtypeStruct((tiles, height, size), jnp.float32),
        in_specs=[SMEM] + [VMEM] * 5,
        out_specs=VMEM,
        scratch_shapes=[pltpu.VMEM((tiles, height, size), jnp.bfloat16)],
        cost_estimate=cost(tiles * NEAR * size * size, 160),
        name="near_walk",
    )(table, pool, prior, inverse, projection, kernel_half)


def far_walk_body(
    tiles, far, inverse, projection, kernel_half, partial, raw, half, degree, gram, scaled
):
    size = far.shape[2]
    columns = projection.shape[0]
    far_slots = kernel_half.shape[1]
    gram[...] = jnp.zeros_like(gram)

    def prepare(index, carry):
        main, extra = scale_start(
            projection[...],
            far[index, 0:size, :],
            far[index, size + 1 : size + 2, :].astype(jnp.float32),
            inverse[index],
        )
        scaled[index, 0:columns, :] = main
        scaled[index, columns : columns + 16, :] = extra
        return carry

    lax.fori_loop(0, far.shape[0], prepare, 0, unroll=4)

    def one_tile(tile, carry):
        total = partial[tile]
        for slot in range(far_slots):
            total = total + jnp.dot(
                scaled[tile * far_slots + slot],
                kernel_half[tile, slot],
                preferred_element_type=jnp.float32,
            )
        below = total[columns : columns + 1] + total[columns + 1 : columns + 2]
        degree[tile] = below
        value = total[0:columns] / below
        raw[:, pl.ds(pl.multiple_of(tile * size, size), size)] = value
        half[tile] = value.astype(jnp.bfloat16)
        return carry

    lax.fori_loop(0, tiles, one_tile, 0, unroll=2)
    gram[...] = nt_dot(raw[...], raw[...], lax.Precision.HIGHEST)


def far_walk(far, inverse, projection, kernel_half, partial):
    tiles, _, size, _ = kernel_half.shape
    columns = projection.shape[0]
    return pl.pallas_call(
        functools.partial(far_walk_body, tiles),
        out_shape=(
            jax.ShapeDtypeStruct((columns, tiles * size), jnp.float32),
            jax.ShapeDtypeStruct((tiles, columns, size), jnp.bfloat16),
            jax.ShapeDtypeStruct((tiles, 1, size), jnp.float32),
            jax.ShapeDtypeStruct((columns, columns), jnp.float32),
        ),
        in_specs=[VMEM] * 5,
        out_specs=(VMEM,) * 4,
        scratch_shapes=[pltpu.VMEM((far.shape[0], columns + 16, size), jnp.bfloat16)],
        name="far_walk",
    )(far, inverse, projection, kernel_half, partial)


def lower_inverse_of(gram, total_rows):
    count = gram.shape[0]
    row = lax.broadcasted_iota(jnp.int32, (count, 2 * count), 0)
    lane = lax.broadcasted_iota(jnp.int32, (count, 2 * count), 1)
    identity = jnp.where(row == lane, 1.0, 0.0)[:, 0:count]
    work = jnp.concatenate([identity, gram * (1.0 / total_rows)], axis=1)
    for step in range(count - 1):
        at = count + step
        factor = work[:, at : at + 1] / work[step : step + 1, at : at + 1]
        below = jnp.where(row[:, 0:1] > step, factor, 0.0)
        work = work - below * work[step : step + 1, :]
    pivots = jnp.sum(jnp.where(lane == row + count, work, 0.0), axis=1, keepdims=True)
    return work[:, 0:count] / jnp.sqrt(pivots)


def finish_body(total_rows, gram, raw, basis):
    basis[...] = jnp.dot(
        lower_inverse_of(gram[...], total_rows),
        raw[...],
        precision=lax.Precision.HIGHEST,
        preferred_element_type=jnp.float32,
    )


def finish(gram, raw, total_rows):
    return pl.pallas_call(
        functools.partial(finish_body, total_rows),
        out_shape=jax.ShapeDtypeStruct(raw.shape, jnp.float32),
        in_specs=[VMEM, VMEM],
        out_specs=VMEM,
        name="finish",
    )(gram, raw)


def near_apply_body(
    tiles, slots, total_rows, table, gram, raw, inverse, kernel_half, basis, partial, lower, scaled
):
    size = inverse.shape[2]
    lower[...] = lower_inverse_of(gram[...], total_rows)
    value = jnp.dot(
        lower[...],
        raw[...],
        precision=lax.Precision.HIGHEST,
        preferred_element_type=jnp.float32,
    )
    basis[...] = value
    for tile in range(tiles):
        part = value[:, tile * size : (tile + 1) * size]
        scaled[tile] = (part * inverse[tile]).astype(jnp.bfloat16)

    def one_tile(tile, carry):
        total = jnp.zeros(partial.shape[1:], jnp.float32)
        for slot in range(NEAR):
            total = total + jnp.dot(
                scaled[table[tile * slots + slot]],
                kernel_half[tile, slot],
                preferred_element_type=jnp.float32,
            )
        partial[tile] = total
        return carry

    lax.fori_loop(0, tiles, one_tile, 0)


def near_apply(table, gram, raw, inverse, kernel_half, slots, total_rows):
    tiles, _, size, _ = kernel_half.shape
    columns = raw.shape[0]
    return pl.pallas_call(
        functools.partial(near_apply_body, tiles, slots, total_rows),
        out_shape=(
            jax.ShapeDtypeStruct(raw.shape, jnp.float32),
            jax.ShapeDtypeStruct((tiles, columns, size), jnp.float32),
            jax.ShapeDtypeStruct(gram.shape, jnp.float32),
        ),
        in_specs=[SMEM] + [VMEM] * 4,
        out_specs=(VMEM, VMEM, VMEM),
        scratch_shapes=[pltpu.VMEM((tiles, columns, size), jnp.bfloat16)],
        cost_estimate=cost(tiles * NEAR * size * size, 128),
        name="near_apply",
    )(table, gram, raw, inverse, kernel_half)


def far_apply_body(tiles, lower_inverse, far, inverse, degree, kernel_half, partial, raw, gram, scaled):
    size = far.shape[2]
    far_slots = kernel_half.shape[1]

    def prepare(index, carry):
        basis = jnp.dot(
            lower_inverse[...],
            far[index].astype(jnp.float32),
            precision=lax.Precision.HIGHEST,
            preferred_element_type=jnp.float32,
        )
        scaled[index] = (basis * inverse[index]).astype(jnp.bfloat16)
        return carry

    lax.fori_loop(0, far.shape[0], prepare, 0, unroll=4)

    def one_tile(tile, carry):
        total = partial[tile]
        for slot in range(far_slots):
            total = total + jnp.dot(
                scaled[tile * far_slots + slot],
                kernel_half[tile, slot],
                preferred_element_type=jnp.float32,
            )
        raw[:, pl.ds(pl.multiple_of(tile * size, size), size)] = total / degree[tile]
        return carry

    lax.fori_loop(0, tiles, one_tile, 0, unroll=2)
    gram[...] = nt_dot(raw[...], raw[...], lax.Precision.HIGHEST)


def far_apply(lower_inverse, far, inverse, degree, kernel_half, partial):
    tiles, columns, size = partial.shape
    return pl.pallas_call(
        functools.partial(far_apply_body, tiles),
        out_shape=(
            jax.ShapeDtypeStruct((columns, tiles * size), jnp.float32),
            jax.ShapeDtypeStruct((columns, columns), jnp.float32),
        ),
        in_specs=[VMEM] * 6,
        out_specs=(VMEM, VMEM),
        scratch_shapes=[pltpu.VMEM(far.shape, jnp.bfloat16)],
        name="far_apply",
    )(lower_inverse, far, inverse, degree, kernel_half, partial)


def exchange(count, peer, me, source, target, send, recv):
    def copy(step, mine):
        other, device = peer(step)
        slot = me if mine else other
        return pltpu.make_async_remote_copy(
            src_ref=source(other),
            dst_ref=target.at[slot],
            send_sem=send.at[other],
            recv_sem=recv.at[slot],
            device_id=device,
            device_id_type=MESH,
        )

    def start(step, carry):
        copy(step, True).start()
        return carry

    def finish(step, carry):
        copy(step, True).wait_send()
        copy(step, False).wait_recv()
        return carry

    lax.fori_loop(1, count, start, 0)
    lax.fori_loop(1, count, finish, 0)


def greet_all(groups):
    barrier = pltpu.get_barrier_semaphore()
    for count, peer in groups:

        def greet(step, carry):
            pl.semaphore_signal(barrier, inc=1, device_id=peer(step)[1], device_id_type=MESH)
            return carry

        lax.fori_loop(1, count, greet, 0)
    pl.semaphore_wait(barrier, sum(count - 1 for count, _ in groups))


def reduce_body(nz, ny, local, out, parts_w, parts_y, parts_z, stage, sw, rw, sy, ry, sz, rz, sa, ra):
    row = lax.axis_index("rows")
    y = lax.axis_index("grp")
    w = row % PLANE
    z = row // PLANE

    def peer_w(step):
        other = (w + step) % PLANE
        return other, (z * PLANE + other, y)

    def peer_y(step):
        other = (y + step) % ny
        return other, (row, other)

    def peer_z(step):
        other = (z + step) % nz
        return other, (other * PLANE + w, y)

    greet_all(((PLANE, peer_w), (ny, peer_y), (nz, peer_z)))
    exchange(PLANE, peer_w, w, lambda other: local.at[other], parts_w, sw, rw)
    parts_w[w] = local[w]
    stage[0] = jnp.sum(parts_w[...], axis=0)
    exchange(ny, peer_y, y, lambda other: stage.at[0], parts_y, sy, ry)
    parts_y[y] = stage[0]
    stage[1] = jnp.sum(parts_y[...], axis=0)
    exchange(nz, peer_z, z, lambda other: stage.at[1], parts_z, sz, rz)
    parts_z[z] = stage[1]
    stage[2] = jnp.sum(parts_z[...], axis=0)
    exchange(PLANE, peer_w, w, lambda other: stage.at[2], out, sa, ra)
    out[w] = stage[2]


def request_body(nz, wanted, got, parts, sw, rw, sz, rz):
    row = lax.axis_index("rows")
    y = lax.axis_index("grp")
    w = row % PLANE
    z = row // PLANE

    def peer_w(step):
        other = (w + step) % PLANE
        return other, (z * PLANE + other, y)

    def peer_z(step):
        other = (z + step) % nz
        return other, (other * PLANE + w, y)

    greet_all(((PLANE, peer_w), (nz, peer_z)))
    exchange(PLANE, peer_w, w, lambda other: wanted.at[other], parts, sw, rw)
    parts[w] = wanted[w]
    exchange(nz, peer_z, z, lambda other: parts, got, sz, rz)
    got[z] = parts[...]


def swap_requests(wanted):
    nrows = wanted.shape[0]
    nz = nrows // PLANE
    dma = pltpu.SemaphoreType.DMA
    sent = jnp.pad(wanted.reshape(nz, PLANE).T, ((0, 0), (0, 128 - nz)))[:, None, :]
    got = pl.pallas_call(
        functools.partial(request_body, nz),
        out_shape=jax.ShapeDtypeStruct((nz,) + sent.shape, sent.dtype),
        in_specs=[VMEM],
        out_specs=VMEM,
        scratch_shapes=[
            pltpu.VMEM(sent.shape, sent.dtype),
            dma((PLANE,)),
            dma((PLANE,)),
            dma((nz,)),
            dma((nz,)),
        ],
        compiler_params=pltpu.CompilerParams(collective_id=1, has_side_effects=True),
        name="swap_requests",
    )(sent)
    z = lax.axis_index("rows") // PLANE
    return lax.dynamic_index_in_dim(got, z, axis=3, keepdims=False).reshape(nrows)


def total_gram(gram):
    columns = gram.shape[0]
    height = columns // PLANE
    ny = lax.axis_size("grp")
    nz = lax.axis_size("rows") // PLANE
    chunk = (height, columns)
    dma = pltpu.SemaphoreType.DMA
    out = pl.pallas_call(
        functools.partial(reduce_body, nz, ny),
        out_shape=jax.ShapeDtypeStruct((PLANE,) + chunk, jnp.float32),
        in_specs=[VMEM],
        out_specs=VMEM,
        scratch_shapes=[
            pltpu.VMEM((PLANE,) + chunk, jnp.float32),
            pltpu.VMEM((ny,) + chunk, jnp.float32),
            pltpu.VMEM((nz,) + chunk, jnp.float32),
            pltpu.VMEM((3,) + chunk, jnp.float32),
            dma((PLANE,)),
            dma((PLANE,)),
            dma((ny,)),
            dma((ny,)),
            dma((nz,)),
            dma((nz,)),
            dma((PLANE,)),
            dma((PLANE,)),
        ],
        compiler_params=pltpu.CompilerParams(collective_id=0, has_side_effects=True),
        name="gram_reduce",
    )(gram.reshape((PLANE,) + chunk))
    return out.reshape(columns, columns)


def exchange_tiles(tiles, requested, owner):
    sent = jnp.take(tiles, requested, axis=0, mode="clip")
    got = lax.all_to_all(sent, "rows", split_axis=0, concat_axis=0, tiled=True)
    return jnp.take(got, owner, axis=0, mode="clip")


def shards(features, length_scale, prior, partners, counts, projection):
    tiles, slots = partners.shape[1:]
    size = features.shape[1] // tiles
    columns = projection.shape[1]
    nrows = lax.axis_size("rows")
    device_index = lax.axis_index("rows")
    own_rows = features[0].reshape(tiles, size, features.shape[2])
    own_side = jnp.stack(
        [length_scale[0].reshape(tiles, size), prior[0].reshape(tiles, size)], axis=1
    )
    lists = partners[0]
    far_tiles = lists[:, NEAR:].reshape(-1)
    owner = far_tiles // tiles
    hits = owner[:, None] == jnp.arange(nrows, dtype=jnp.int32)[None, :]
    wanted = jnp.sum(jnp.where(hits, (far_tiles % tiles)[:, None], 0), axis=0)
    requested = swap_requests(wanted)
    table = (lists - device_index * tiles).reshape(-1)

    far = exchange_tiles(jnp.concatenate([own_rows, own_side], axis=1), requested, owner)
    side = own_side.astype(jnp.float32)
    own_band, own_prior = side[:, 0:1, :], side[:, 1:2, :]
    directions = projection.T
    near_half, near_density, norms = near_kernel(table, counts[0], own_rows, own_band, slots)
    far_half, own_inverse = far_kernel(
        counts[0], own_rows, own_band, far, norms, near_density, slots
    )
    far_inverse = exchange_tiles(own_inverse.astype(jnp.bfloat16), requested, owner)
    far_inverse = far_inverse.astype(jnp.float32)
    near_part = near_walk(table, own_rows, own_prior, own_inverse, directions, near_half, slots)
    raw, raw_half, degree, gram = far_walk(
        far, far_inverse, directions, far_half, near_part
    )
    gram, raw_half = lax.optimization_barrier((total_gram(gram), raw_half))
    far_raw = exchange_tiles(raw_half, requested, owner)
    total_rows = nrows * lax.axis_size("grp") * tiles * size
    basis, near_second, lower_inverse = near_apply(
        table, gram, raw, own_inverse, near_half, slots, total_rows
    )
    second_raw, second_gram = far_apply(
        lower_inverse, far_raw, far_inverse, degree, far_half, near_second
    )
    embedding = finish(total_gram(second_gram), second_raw, total_rows)
    return basis[None], embedding[None]


def solution(mesh):
    in_specs = (
        P("grp", "rows", None),
        P("grp", "rows"),
        P("grp", "rows"),
        P("grp", "rows", None),
        P("grp", "rows"),
        P(),
    )
    out_specs = (P("grp", None, "rows"), P("grp", None, "rows"))
    return jax.shard_map(shards, mesh=mesh, in_specs=in_specs, out_specs=out_specs, check_vma=False)
```

```python
import functools

import jax
import jax.numpy as jnp
from jax import lax
from jax.experimental import pallas as pl
from jax.experimental.pallas import tpu as pltpu
from jax.sharding import PartitionSpec as P

NEAR = 13
PLANE = 8
MESH = pl.DeviceIdType.MESH
VMEM = pl.BlockSpec(memory_space=pltpu.VMEM)
SMEM = pl.BlockSpec(memory_space=pltpu.SMEM)


def nt_dot(left, right, precision=None):
    return lax.dot_general(
        left,
        right,
        (((1,), (1,)), ((), ())),
        precision=precision,
        preferred_element_type=jnp.float32,
    )


def load_norm(rows):
    wide = rows.astype(jnp.float32)
    norm = jnp.sum(wide * wide, axis=1, keepdims=True)
    return jnp.broadcast_to(-norm, (rows.shape[0], rows.shape[0]))


def column_band(row):
    return jnp.transpose(jnp.broadcast_to(row, (row.shape[1], row.shape[1])))


def kernel_value(rows, norm, band, doubled, own_norm, own_band):
    level = jnp.minimum(nt_dot(rows, doubled) + (norm + own_norm), 0.0)
    return jnp.exp(level / (band + own_band))


def fold_rows(value):
    return jnp.sum(value.reshape(value.shape[0] // 8, 8, value.shape[1]), axis=0)


def near_kernel_body(
    tiles, slots, table, counts, pool, band, kernel_half, density, norm_a, norm_b, band_b
):
    size = pool.shape[1]

    def prepare(index, carry):
        wide = load_norm(pool[index])
        norm_b[index] = wide
        band_b[index] = column_band(band[index])
        norm_a[index] = jnp.transpose(wide)[0:1, :]
        return carry

    lax.fori_loop(0, tiles, prepare, 0)

    def one_tile(tile, carry):
        doubled = pool[tile] * jnp.bfloat16(2)
        own_norm = norm_a[tile]
        own_band = band[tile]
        live = counts[tile]
        total = jnp.zeros((8, size), jnp.float32)
        for slot in range(NEAR):
            index = table[tile * slots + slot]
            value = kernel_value(
                pool[index], norm_b[index], band_b[index], doubled, own_norm, own_band
            )
            if slot == NEAR - 1:
                value = jnp.where(slot < live, value, 0.0)
            kernel_half[tile, slot] = value.astype(jnp.bfloat16)
            total = total + fold_rows(value)
        density[tile] = jnp.sum(total, axis=0, keepdims=True)
        return carry

    lax.fori_loop(0, tiles, one_tile, 0)


def near_kernel(table, counts, pool, band, slots):
    tiles, size, _ = pool.shape
    return pl.pallas_call(
        functools.partial(near_kernel_body, tiles, slots),
        out_shape=(
            jax.ShapeDtypeStruct((tiles, NEAR, size, size), jnp.bfloat16),
            jax.ShapeDtypeStruct((tiles, 1, size), jnp.float32),
            jax.ShapeDtypeStruct((tiles, 1, size), jnp.float32),
        ),
        in_specs=[SMEM, SMEM, VMEM, VMEM],
        out_specs=(VMEM, VMEM, VMEM),
        scratch_shapes=[pltpu.VMEM((tiles, size, size), jnp.float32)] * 2,
        cost_estimate=cost(tiles * NEAR * size * size, 400),
        name="near_kernel",
    )(table, counts, pool, band)


def far_kernel_body(tiles, slots, counts, pool, band, far, norm_a, near, kernel_half, inverse):
    far_slots = slots - NEAR
    size = pool.shape[1]

    def one_tile(tile, carry):
        doubled = pool[tile] * jnp.bfloat16(2)
        live = counts[tile]
        total = jnp.zeros((8, pool.shape[1]), jnp.float32)
        for slot in range(far_slots):
            index = tile * far_slots + slot
            rows = far[index, 0:size, :]
            value = kernel_value(
                rows,
                load_norm(rows),
                column_band(far[index, size : size + 1, :].astype(jnp.float32)),
                doubled,
                norm_a[tile],
                band[tile],
            )
            value = jnp.where(slot + NEAR < live, value, 0.0)
            kernel_half[tile, slot] = value.astype(jnp.bfloat16)
            total = total + fold_rows(value)
        inverse[tile] = 1.0 / (near[tile] + jnp.sum(total, axis=0, keepdims=True))
        return carry

    lax.fori_loop(0, tiles, one_tile, 0, unroll=2)


def far_kernel(counts, pool, band, far, norm_a, near, slots):
    tiles, size, _ = pool.shape
    return pl.pallas_call(
        functools.partial(far_kernel_body, tiles, slots),
        out_shape=(
            jax.ShapeDtypeStruct((tiles, slots - NEAR, size, size), jnp.bfloat16),
            jax.ShapeDtypeStruct((tiles, 1, size), jnp.float32),
        ),
        in_specs=[SMEM] + [VMEM] * 5,
        out_specs=(VMEM, VMEM),
        name="far_kernel",
    )(counts, pool, band, far, norm_a, near)


def cost(flops, scale):
    return pl.CostEstimate(flops=flops * scale, bytes_accessed=flops * 4, transcendentals=flops)


def scale_start(projection, rows, prior, inv):
    start = nt_dot(projection, rows)
    scaled = (start * (prior * inv)).astype(jnp.bfloat16)
    high = inv.astype(jnp.bfloat16).astype(jnp.float32)
    row = lax.broadcasted_iota(jnp.int32, (16, inv.shape[1]), 0)
    extra = jnp.where(row == 0, high, jnp.where(row == 1, inv - high, 0.0))
    return scaled, extra.astype(jnp.bfloat16)


def near_walk_body(
    tiles, slots, table, pool, prior, inverse, projection, kernel_half, partial, scaled
):
    columns = projection.shape[0]

    def prepare(index, carry):
        main, extra = scale_start(projection[...], pool[index], prior[index], inverse[index])
        scaled[index, 0:columns, :] = main
        scaled[index, columns : columns + 16, :] = extra
        return carry

    lax.fori_loop(0, tiles, prepare, 0, unroll=2)

    def one_tile(tile, carry):
        total = jnp.zeros(partial.shape[1:], jnp.float32)
        for slot in range(NEAR):
            total = total + jnp.dot(
                scaled[table[tile * slots + slot]],
                kernel_half[tile, slot],
                preferred_element_type=jnp.float32,
            )
        partial[tile] = total
        return carry

    lax.fori_loop(0, tiles, one_tile, 0)


def near_walk(table, pool, prior, inverse, projection, kernel_half, slots):
    tiles, _, size, _ = kernel_half.shape
    height = projection.shape[0] + 16
    return pl.pallas_call(
        functools.partial(near_walk_body, tiles, slots),
        out_shape=jax.ShapeDtypeStruct((tiles, height, size), jnp.float32),
        in_specs=[SMEM] + [VMEM] * 5,
        out_specs=VMEM,
        scratch_shapes=[pltpu.VMEM((tiles, height, size), jnp.bfloat16)],
        cost_estimate=cost(tiles * NEAR * size * size, 160),
        name="near_walk",
    )(table, pool, prior, inverse, projection, kernel_half)


def far_walk_body(
    tiles, far, inverse, projection, kernel_half, partial, raw, half, degree, gram, scaled
):
    size = far.shape[2]
    columns = projection.shape[0]
    far_slots = kernel_half.shape[1]
    gram[...] = jnp.zeros_like(gram)

    def prepare(index, carry):
        main, extra = scale_start(
            projection[...],
            far[index, 0:size, :],
            far[index, size + 1 : size + 2, :].astype(jnp.float32),
            inverse[index],
        )
        scaled[index, 0:columns, :] = main
        scaled[index, columns : columns + 16, :] = extra
        return carry

    lax.fori_loop(0, far.shape[0], prepare, 0, unroll=4)

    def one_tile(tile, carry):
        total = partial[tile]
        for slot in range(far_slots):
            total = total + jnp.dot(
                scaled[tile * far_slots + slot],
                kernel_half[tile, slot],
                preferred_element_type=jnp.float32,
            )
        below = total[columns : columns + 1] + total[columns + 1 : columns + 2]
        degree[tile] = below
        value = total[0:columns] / below
        raw[:, pl.ds(pl.multiple_of(tile * size, size), size)] = value
        half[tile] = value.astype(jnp.bfloat16)
        return carry

    lax.fori_loop(0, tiles, one_tile, 0, unroll=2)
    gram[...] = nt_dot(raw[...], raw[...], lax.Precision.HIGHEST)


def far_walk(far, inverse, projection, kernel_half, partial):
    tiles, _, size, _ = kernel_half.shape
    columns = projection.shape[0]
    return pl.pallas_call(
        functools.partial(far_walk_body, tiles),
        out_shape=(
            jax.ShapeDtypeStruct((columns, tiles * size), jnp.float32),
            jax.ShapeDtypeStruct((tiles, columns, size), jnp.bfloat16),
            jax.ShapeDtypeStruct((tiles, 1, size), jnp.float32),
            jax.ShapeDtypeStruct((columns, columns), jnp.float32),
        ),
        in_specs=[VMEM] * 5,
        out_specs=(VMEM,) * 4,
        scratch_shapes=[pltpu.VMEM((far.shape[0], columns + 16, size), jnp.bfloat16)],
        name="far_walk",
    )(far, inverse, projection, kernel_half, partial)


def lower_inverse_of(gram, total_rows):
    count = gram.shape[0]
    row = lax.broadcasted_iota(jnp.int32, (count, 2 * count), 0)
    lane = lax.broadcasted_iota(jnp.int32, (count, 2 * count), 1)
    identity = jnp.where(row == lane, 1.0, 0.0)[:, 0:count]
    work = jnp.concatenate([identity, gram * (1.0 / total_rows)], axis=1)
    for step in range(count - 1):
        at = count + step
        factor = work[:, at : at + 1] / work[step : step + 1, at : at + 1]
        below = jnp.where(row[:, 0:1] > step, factor, 0.0)
        work = work - below * work[step : step + 1, :]
    pivots = jnp.sum(jnp.where(lane == row + count, work, 0.0), axis=1, keepdims=True)
    return work[:, 0:count] / jnp.sqrt(pivots)


def finish_body(total_rows, gram, raw, basis):
    basis[...] = jnp.dot(
        lower_inverse_of(gram[...], total_rows),
        raw[...],
        precision=lax.Precision.HIGHEST,
        preferred_element_type=jnp.float32,
    )


def finish(gram, raw, total_rows):
    return pl.pallas_call(
        functools.partial(finish_body, total_rows),
        out_shape=jax.ShapeDtypeStruct(raw.shape, jnp.float32),
        in_specs=[VMEM, VMEM],
        out_specs=VMEM,
        name="finish",
    )(gram, raw)


def near_apply_body(
    tiles, slots, total_rows, table, gram, raw, inverse, kernel_half, basis, partial, lower, scaled
):
    size = inverse.shape[2]
    lower[...] = lower_inverse_of(gram[...], total_rows)
    value = jnp.dot(
        lower[...],
        raw[...],
        precision=lax.Precision.HIGHEST,
        preferred_element_type=jnp.float32,
    )
    basis[...] = value
    for tile in range(tiles):
        part = value[:, tile * size : (tile + 1) * size]
        scaled[tile] = (part * inverse[tile]).astype(jnp.bfloat16)

    def one_tile(tile, carry):
        total = jnp.zeros(partial.shape[1:], jnp.float32)
        for slot in range(NEAR):
            total = total + jnp.dot(
                scaled[table[tile * slots + slot]],
                kernel_half[tile, slot],
                preferred_element_type=jnp.float32,
            )
        partial[tile] = total
        return carry

    lax.fori_loop(0, tiles, one_tile, 0)


def near_apply(table, gram, raw, inverse, kernel_half, slots, total_rows):
    tiles, _, size, _ = kernel_half.shape
    columns = raw.shape[0]
    return pl.pallas_call(
        functools.partial(near_apply_body, tiles, slots, total_rows),
        out_shape=(
            jax.ShapeDtypeStruct(raw.shape, jnp.float32),
            jax.ShapeDtypeStruct((tiles, columns, size), jnp.float32),
            jax.ShapeDtypeStruct(gram.shape, jnp.float32),
        ),
        in_specs=[SMEM] + [VMEM] * 4,
        out_specs=(VMEM, VMEM, VMEM),
        scratch_shapes=[pltpu.VMEM((tiles, columns, size), jnp.bfloat16)],
        cost_estimate=cost(tiles * NEAR * size * size, 128),
        name="near_apply",
    )(table, gram, raw, inverse, kernel_half)


def far_apply_body(tiles, lower_inverse, far, inverse, degree, kernel_half, partial, raw, gram, scaled):
    size = far.shape[2]
    far_slots = kernel_half.shape[1]

    def prepare(index, carry):
        basis = jnp.dot(
            lower_inverse[...],
            far[index].astype(jnp.float32),
            precision=lax.Precision.HIGHEST,
            preferred_element_type=jnp.float32,
        )
        scaled[index] = (basis * inverse[index]).astype(jnp.bfloat16)
        return carry

    lax.fori_loop(0, far.shape[0], prepare, 0, unroll=4)

    def one_tile(tile, carry):
        total = partial[tile]
        for slot in range(far_slots):
            total = total + jnp.dot(
                scaled[tile * far_slots + slot],
                kernel_half[tile, slot],
                preferred_element_type=jnp.float32,
            )
        raw[:, pl.ds(pl.multiple_of(tile * size, size), size)] = total / degree[tile]
        return carry

    lax.fori_loop(0, tiles, one_tile, 0, unroll=2)
    gram[...] = nt_dot(raw[...], raw[...], lax.Precision.HIGHEST)


def far_apply(lower_inverse, far, inverse, degree, kernel_half, partial):
    tiles, columns, size = partial.shape
    return pl.pallas_call(
        functools.partial(far_apply_body, tiles),
        out_shape=(
            jax.ShapeDtypeStruct((columns, tiles * size), jnp.float32),
            jax.ShapeDtypeStruct((columns, columns), jnp.float32),
        ),
        in_specs=[VMEM] * 6,
        out_specs=(VMEM, VMEM),
        scratch_shapes=[pltpu.VMEM(far.shape, jnp.bfloat16)],
        name="far_apply",
    )(lower_inverse, far, inverse, degree, kernel_half, partial)


def exchange(count, peer, me, source, target, send, recv):
    def copy(step, mine):
        other, device = peer(step)
        slot = me if mine else other
        return pltpu.make_async_remote_copy(
            src_ref=source(other),
            dst_ref=target.at[slot],
            send_sem=send.at[other],
            recv_sem=recv.at[slot],
            device_id=device,
            device_id_type=MESH,
        )

    def start(step, carry):
        copy(step, True).start()
        return carry

    def finish(step, carry):
        copy(step, True).wait_send()
        copy(step, False).wait_recv()
        return carry

    lax.fori_loop(1, count, start, 0)
    lax.fori_loop(1, count, finish, 0)


def greet_all(groups):
    barrier = pltpu.get_barrier_semaphore()
    for count, peer in groups:

        def greet(step, carry):
            pl.semaphore_signal(barrier, inc=1, device_id=peer(step)[1], device_id_type=MESH)
            return carry

        lax.fori_loop(1, count, greet, 0)
    pl.semaphore_wait(barrier, sum(count - 1 for count, _ in groups))


def reduce_body(nz, ny, local, total, chunks, parts, parts_z, sums, gathered, sp, rp, sz, rz, sa, ra):
    row = lax.axis_index("rows")
    y = lax.axis_index("grp")
    w = row % PLANE
    z = row // PLANE
    count = PLANE * ny
    me = y * PLANE + w
    height = local.shape[0] // count

    def peer_p(step):
        other = (me + step) % count
        return other, (z * PLANE + other % PLANE, other // PLANE)

    def peer_z(step):
        other = (z + step) % nz
        return other, (other * PLANE + w, y)

    for index in range(count):
        chunks[index] = local[index * height : (index + 1) * height, :]
    greet_all(((count, peer_p), (nz, peer_z)))
    exchange(count, peer_p, me, lambda other: chunks.at[other], parts, sp, rp)
    parts[me] = chunks[me]
    sums[0] = jnp.sum(parts[...], axis=0)
    exchange(nz, peer_z, z, lambda other: sums.at[0], parts_z, sz, rz)
    parts_z[z] = sums[0]
    sums[1] = jnp.sum(parts_z[...], axis=0)
    exchange(count, peer_p, me, lambda other: sums.at[1], gathered, sa, ra)
    gathered[me] = sums[1]
    for index in range(count):
        total[index * height : (index + 1) * height, :] = gathered[index]


def total_gram(gram):
    columns = gram.shape[0]
    ny = lax.axis_size("grp")
    nz = lax.axis_size("rows") // PLANE
    count = PLANE * ny
    chunk = (columns // count, columns)
    dma = pltpu.SemaphoreType.DMA
    return pl.pallas_call(
        functools.partial(reduce_body, nz, ny),
        out_shape=jax.ShapeDtypeStruct(gram.shape, jnp.float32),
        in_specs=[VMEM],
        out_specs=VMEM,
        scratch_shapes=[
            pltpu.VMEM((count,) + chunk, jnp.float32),
            pltpu.VMEM((count,) + chunk, jnp.float32),
            pltpu.VMEM((nz,) + chunk, jnp.float32),
            pltpu.VMEM((2,) + chunk, jnp.float32),
            pltpu.VMEM((count,) + chunk, jnp.float32),
            dma((count,)),
            dma((count,)),
            dma((nz,)),
            dma((nz,)),
            dma((count,)),
            dma((count,)),
        ],
        compiler_params=pltpu.CompilerParams(collective_id=0, has_side_effects=True),
        name="gram_reduce",
    )(gram)


def request_body(nz, wanted, got, parts, sw, rw, sz, rz):
    row = lax.axis_index("rows")
    y = lax.axis_index("grp")
    w = row % PLANE
    z = row // PLANE

    def peer_w(step):
        other = (w + step) % PLANE
        return other, (z * PLANE + other, y)

    def peer_z(step):
        other = (z + step) % nz
        return other, (other * PLANE + w, y)

    greet_all(((PLANE, peer_w), (nz, peer_z)))
    exchange(PLANE, peer_w, w, lambda other: wanted.at[other], parts, sw, rw)
    parts[w] = wanted[w]
    exchange(nz, peer_z, z, lambda other: parts, got, sz, rz)
    got[z] = parts[...]


def swap_requests(wanted):
    nrows = wanted.shape[0]
    nz = nrows // PLANE
    dma = pltpu.SemaphoreType.DMA
    sent = jnp.pad(wanted.reshape(nz, PLANE).T, ((0, 0), (0, 128 - nz)))[:, None, :]
    got = pl.pallas_call(
        functools.partial(request_body, nz),
        out_shape=jax.ShapeDtypeStruct((nz,) + sent.shape, sent.dtype),
        in_specs=[VMEM],
        out_specs=VMEM,
        scratch_shapes=[
            pltpu.VMEM(sent.shape, sent.dtype),
            dma((PLANE,)),
            dma((PLANE,)),
            dma((nz,)),
            dma((nz,)),
        ],
        compiler_params=pltpu.CompilerParams(collective_id=1, has_side_effects=True),
        name="swap_requests",
    )(sent)
    z = lax.axis_index("rows") // PLANE
    return lax.dynamic_index_in_dim(got, z, axis=3, keepdims=False).reshape(nrows)


def exchange_tiles(tiles, requested, owner):
    sent = jnp.take(tiles, requested, axis=0, mode="clip")
    got = lax.all_to_all(sent, "rows", split_axis=0, concat_axis=0, tiled=True)
    return jnp.take(got, owner, axis=0, mode="clip")


def shards(features, length_scale, prior, partners, counts, projection):
    tiles, slots = partners.shape[1:]
    size = features.shape[1] // tiles
    columns = projection.shape[1]
    nrows = lax.axis_size("rows")
    device_index = lax.axis_index("rows")
    own_rows = features[0].reshape(tiles, size, features.shape[2])
    own_side = jnp.stack(
        [length_scale[0].reshape(tiles, size), prior[0].reshape(tiles, size)], axis=1
    )
    lists = partners[0]
    far_tiles = lists[:, NEAR:].reshape(-1)
    owner = far_tiles // tiles
    hits = owner[:, None] == jnp.arange(nrows, dtype=jnp.int32)[None, :]
    wanted = jnp.sum(jnp.where(hits, (far_tiles % tiles)[:, None], 0), axis=0)
    requested = swap_requests(wanted)
    table = (lists - device_index * tiles).reshape(-1)

    packed = jnp.concatenate([own_rows, own_side], axis=1).reshape(tiles, 2, -1)
    far = exchange_tiles(packed, requested, owner).reshape(owner.shape[0], size + 2, -1)
    side = own_side.astype(jnp.float32)
    own_band, own_prior = side[:, 0:1, :], side[:, 1:2, :]
    directions = projection.T
    near_half, near_density, norms = near_kernel(table, counts[0], own_rows, own_band, slots)
    far_half, own_inverse = far_kernel(
        counts[0], own_rows, own_band, far, norms, near_density, slots
    )
    far_inverse = exchange_tiles(own_inverse.astype(jnp.bfloat16), requested, owner)
    far_inverse = far_inverse.astype(jnp.float32)
    near_part = near_walk(table, own_rows, own_prior, own_inverse, directions, near_half, slots)
    raw, raw_half, degree, gram = far_walk(
        far, far_inverse, directions, far_half, near_part
    )
    gram, raw_half = lax.optimization_barrier((total_gram(gram), raw_half))
    far_raw = exchange_tiles(raw_half, requested, owner)
    total_rows = nrows * lax.axis_size("grp") * tiles * size
    basis, near_second, lower_inverse = near_apply(
        table, gram, raw, own_inverse, near_half, slots, total_rows
    )
    second_raw, second_gram = far_apply(
        lower_inverse, far_raw, far_inverse, degree, far_half, near_second
    )
    embedding = finish(total_gram(second_gram), second_raw, total_rows)
    return basis[None], embedding[None]


def solution(mesh):
    in_specs = (
        P("grp", "rows", None),
        P("grp", "rows"),
        P("grp", "rows"),
        P("grp", "rows", None),
        P("grp", "rows"),
        P(),
    )
    out_specs = (P("grp", None, "rows"), P("grp", None, "rows"))
    return jax.shard_map(shards, mesh=mesh, in_specs=in_specs, out_specs=out_specs, check_vma=False)
```

```python
import functools

import jax
import jax.numpy as jnp
from jax import lax
from jax.experimental import pallas as pl
from jax.experimental.pallas import tpu as pltpu
from jax.sharding import PartitionSpec as P

NEAR = 13
PLANE = 8
MESH = pl.DeviceIdType.MESH
VMEM = pl.BlockSpec(memory_space=pltpu.VMEM)
SMEM = pl.BlockSpec(memory_space=pltpu.SMEM)


def nt_dot(left, right, precision=None):
    return lax.dot_general(
        left,
        right,
        (((1,), (1,)), ((), ())),
        precision=precision,
        preferred_element_type=jnp.float32,
    )


def load_norm(rows):
    wide = rows.astype(jnp.float32)
    norm = jnp.sum(wide * wide, axis=1, keepdims=True)
    return jnp.broadcast_to(-norm, (rows.shape[0], rows.shape[0]))


def column_band(row):
    return jnp.transpose(jnp.broadcast_to(row, (row.shape[1], row.shape[1])))


def kernel_value(rows, norm, band, doubled, own_norm, own_band):
    level = jnp.minimum(nt_dot(rows, doubled) + (norm + own_norm), 0.0)
    return jnp.exp(level / (band + own_band))


def fold_rows(value):
    return jnp.sum(value.reshape(value.shape[0] // 8, 8, value.shape[1]), axis=0)


def near_kernel_body(
    tiles, slots, table, counts, pool, band, kernel_half, density, norm_a, norm_b, band_b
):
    size = pool.shape[1]

    def prepare(index, carry):
        wide = load_norm(pool[index])
        norm_b[index] = wide
        band_b[index] = column_band(band[index])
        norm_a[index] = jnp.transpose(wide)[0:1, :]
        return carry

    lax.fori_loop(0, tiles, prepare, 0)

    def one_tile(tile, carry):
        doubled = pool[tile] * jnp.bfloat16(2)
        own_norm = norm_a[tile]
        own_band = band[tile]
        live = counts[tile]
        total = jnp.zeros((8, size), jnp.float32)
        for slot in range(NEAR):
            index = table[tile * slots + slot]
            value = kernel_value(
                pool[index], norm_b[index], band_b[index], doubled, own_norm, own_band
            )
            if slot == NEAR - 1:
                value = jnp.where(slot < live, value, 0.0)
            kernel_half[tile, slot] = value.astype(jnp.bfloat16)
            total = total + fold_rows(value)
        density[tile] = jnp.sum(total, axis=0, keepdims=True)
        return carry

    lax.fori_loop(0, tiles, one_tile, 0)


def near_kernel(table, counts, pool, band, slots):
    tiles, size, _ = pool.shape
    return pl.pallas_call(
        functools.partial(near_kernel_body, tiles, slots),
        out_shape=(
            jax.ShapeDtypeStruct((tiles, NEAR, size, size), jnp.bfloat16),
            jax.ShapeDtypeStruct((tiles, 1, size), jnp.float32),
            jax.ShapeDtypeStruct((tiles, 1, size), jnp.float32),
        ),
        in_specs=[SMEM, SMEM, VMEM, VMEM],
        out_specs=(VMEM, VMEM, VMEM),
        scratch_shapes=[pltpu.VMEM((tiles, size, size), jnp.float32)] * 2,
        cost_estimate=cost(tiles * NEAR * size * size, 400),
        name="near_kernel",
    )(table, counts, pool, band)


def far_kernel_body(tiles, slots, counts, pool, band, far, norm_a, near, kernel_half, inverse):
    far_slots = slots - NEAR
    size = pool.shape[1]

    def one_tile(tile, carry):
        doubled = pool[tile] * jnp.bfloat16(2)
        live = counts[tile]
        total = jnp.zeros((8, pool.shape[1]), jnp.float32)
        for slot in range(far_slots):
            index = tile * far_slots + slot
            rows = far[index, 0:size, :]
            value = kernel_value(
                rows,
                load_norm(rows),
                column_band(far[index, size : size + 1, :].astype(jnp.float32)),
                doubled,
                norm_a[tile],
                band[tile],
            )
            value = jnp.where(slot + NEAR < live, value, 0.0)
            kernel_half[tile, slot] = value.astype(jnp.bfloat16)
            total = total + fold_rows(value)
        inverse[tile] = 1.0 / (near[tile] + jnp.sum(total, axis=0, keepdims=True))
        return carry

    lax.fori_loop(0, tiles, one_tile, 0, unroll=2)


def far_kernel(counts, pool, band, far, norm_a, near, slots):
    tiles, size, _ = pool.shape
    return pl.pallas_call(
        functools.partial(far_kernel_body, tiles, slots),
        out_shape=(
            jax.ShapeDtypeStruct((tiles, slots - NEAR, size, size), jnp.bfloat16),
            jax.ShapeDtypeStruct((tiles, 1, size), jnp.float32),
        ),
        in_specs=[SMEM] + [VMEM] * 5,
        out_specs=(VMEM, VMEM),
        name="far_kernel",
    )(counts, pool, band, far, norm_a, near)


def cost(flops, scale):
    return pl.CostEstimate(flops=flops * scale, bytes_accessed=flops * 4, transcendentals=flops)


def scale_start(projection, rows, prior, inv):
    start = nt_dot(projection, rows)
    scaled = (start * (prior * inv)).astype(jnp.bfloat16)
    high = inv.astype(jnp.bfloat16).astype(jnp.float32)
    row = lax.broadcasted_iota(jnp.int32, (16, inv.shape[1]), 0)
    extra = jnp.where(row == 0, high, jnp.where(row == 1, inv - high, 0.0))
    return scaled, extra.astype(jnp.bfloat16)


def near_walk_body(
    tiles, slots, table, pool, prior, inverse, projection, kernel_half, partial, scaled
):
    columns = projection.shape[0]

    def prepare(index, carry):
        main, extra = scale_start(projection[...], pool[index], prior[index], inverse[index])
        scaled[index, 0:columns, :] = main
        scaled[index, columns : columns + 16, :] = extra
        return carry

    lax.fori_loop(0, tiles, prepare, 0, unroll=2)

    def one_tile(tile, carry):
        total = jnp.zeros(partial.shape[1:], jnp.float32)
        for slot in range(NEAR):
            total = total + jnp.dot(
                scaled[table[tile * slots + slot]],
                kernel_half[tile, slot],
                preferred_element_type=jnp.float32,
            )
        partial[tile] = total
        return carry

    lax.fori_loop(0, tiles, one_tile, 0)


def near_walk(table, pool, prior, inverse, projection, kernel_half, slots):
    tiles, _, size, _ = kernel_half.shape
    height = projection.shape[0] + 16
    return pl.pallas_call(
        functools.partial(near_walk_body, tiles, slots),
        out_shape=jax.ShapeDtypeStruct((tiles, height, size), jnp.float32),
        in_specs=[SMEM] + [VMEM] * 5,
        out_specs=VMEM,
        scratch_shapes=[pltpu.VMEM((tiles, height, size), jnp.bfloat16)],
        cost_estimate=cost(tiles * NEAR * size * size, 160),
        name="near_walk",
    )(table, pool, prior, inverse, projection, kernel_half)


def far_walk_body(
    tiles, far, inverse, projection, kernel_half, partial, raw, half, degree, gram, scaled
):
    size = far.shape[2]
    columns = projection.shape[0]
    far_slots = kernel_half.shape[1]
    gram[...] = jnp.zeros_like(gram)

    def prepare(index, carry):
        main, extra = scale_start(
            projection[...],
            far[index, 0:size, :],
            far[index, size + 1 : size + 2, :].astype(jnp.float32),
            inverse[index],
        )
        scaled[index, 0:columns, :] = main
        scaled[index, columns : columns + 16, :] = extra
        return carry

    lax.fori_loop(0, far.shape[0], prepare, 0, unroll=4)

    def one_tile(tile, carry):
        total = partial[tile]
        for slot in range(far_slots):
            total = total + jnp.dot(
                scaled[tile * far_slots + slot],
                kernel_half[tile, slot],
                preferred_element_type=jnp.float32,
            )
        below = total[columns : columns + 1] + total[columns + 1 : columns + 2]
        degree[tile] = below
        value = total[0:columns] / below
        raw[:, pl.ds(pl.multiple_of(tile * size, size), size)] = value
        half[tile] = value.astype(jnp.bfloat16)
        return carry

    lax.fori_loop(0, tiles, one_tile, 0, unroll=2)
    gram[...] = nt_dot(raw[...], raw[...], lax.Precision.HIGHEST)


def far_walk(far, inverse, projection, kernel_half, partial):
    tiles, _, size, _ = kernel_half.shape
    columns = projection.shape[0]
    return pl.pallas_call(
        functools.partial(far_walk_body, tiles),
        out_shape=(
            jax.ShapeDtypeStruct((columns, tiles * size), jnp.float32),
            jax.ShapeDtypeStruct((tiles, columns, size), jnp.bfloat16),
            jax.ShapeDtypeStruct((tiles, 1, size), jnp.float32),
            jax.ShapeDtypeStruct((columns, columns), jnp.float32),
        ),
        in_specs=[VMEM] * 5,
        out_specs=(VMEM,) * 4,
        scratch_shapes=[pltpu.VMEM((far.shape[0], columns + 16, size), jnp.bfloat16)],
        name="far_walk",
    )(far, inverse, projection, kernel_half, partial)


def lower_inverse_of(gram, total_rows):
    count = gram.shape[0]
    row = lax.broadcasted_iota(jnp.int32, (count, 2 * count), 0)
    lane = lax.broadcasted_iota(jnp.int32, (count, 2 * count), 1)
    identity = jnp.where(row == lane, 1.0, 0.0)[:, 0:count]
    work = jnp.concatenate([identity, gram * (1.0 / total_rows)], axis=1)
    for step in range(count - 1):
        at = count + step
        factor = work[:, at : at + 1] / work[step : step + 1, at : at + 1]
        below = jnp.where(row[:, 0:1] > step, factor, 0.0)
        work = work - below * work[step : step + 1, :]
    pivots = jnp.sum(jnp.where(lane == row + count, work, 0.0), axis=1, keepdims=True)
    return work[:, 0:count] / jnp.sqrt(pivots)


def finish_body(total_rows, gram, raw, basis):
    basis[...] = jnp.dot(
        lower_inverse_of(gram[...], total_rows),
        raw[...],
        precision=lax.Precision.HIGHEST,
        preferred_element_type=jnp.float32,
    )


def finish(gram, raw, total_rows):
    return pl.pallas_call(
        functools.partial(finish_body, total_rows),
        out_shape=jax.ShapeDtypeStruct(raw.shape, jnp.float32),
        in_specs=[VMEM, VMEM],
        out_specs=VMEM,
        name="finish",
    )(gram, raw)


def near_apply_body(
    tiles, slots, total_rows, table, gram, raw, inverse, kernel_half, basis, partial, lower, scaled
):
    size = inverse.shape[2]
    lower[...] = lower_inverse_of(gram[...], total_rows)
    value = jnp.dot(
        lower[...],
        raw[...],
        precision=lax.Precision.HIGHEST,
        preferred_element_type=jnp.float32,
    )
    basis[...] = value
    for tile in range(tiles):
        part = value[:, tile * size : (tile + 1) * size]
        scaled[tile] = (part * inverse[tile]).astype(jnp.bfloat16)

    def one_tile(tile, carry):
        total = jnp.zeros(partial.shape[1:], jnp.float32)
        for slot in range(NEAR):
            total = total + jnp.dot(
                scaled[table[tile * slots + slot]],
                kernel_half[tile, slot],
                preferred_element_type=jnp.float32,
            )
        partial[tile] = total
        return carry

    lax.fori_loop(0, tiles, one_tile, 0)


def near_apply(table, gram, raw, inverse, kernel_half, slots, total_rows):
    tiles, _, size, _ = kernel_half.shape
    columns = raw.shape[0]
    return pl.pallas_call(
        functools.partial(near_apply_body, tiles, slots, total_rows),
        out_shape=(
            jax.ShapeDtypeStruct(raw.shape, jnp.float32),
            jax.ShapeDtypeStruct((tiles, columns, size), jnp.float32),
            jax.ShapeDtypeStruct(gram.shape, jnp.float32),
        ),
        in_specs=[SMEM] + [VMEM] * 4,
        out_specs=(VMEM, VMEM, VMEM),
        scratch_shapes=[pltpu.VMEM((tiles, columns, size), jnp.bfloat16)],
        cost_estimate=cost(tiles * NEAR * size * size, 128),
        name="near_apply",
    )(table, gram, raw, inverse, kernel_half)


def far_apply_body(tiles, lower_inverse, far, inverse, degree, kernel_half, partial, raw, gram, scaled):
    size = far.shape[2]
    far_slots = kernel_half.shape[1]

    def prepare(index, carry):
        basis = jnp.dot(
            lower_inverse[...],
            far[index].astype(jnp.float32),
            precision=lax.Precision.HIGHEST,
            preferred_element_type=jnp.float32,
        )
        scaled[index] = (basis * inverse[index]).astype(jnp.bfloat16)
        return carry

    lax.fori_loop(0, far.shape[0], prepare, 0, unroll=4)

    def one_tile(tile, carry):
        total = partial[tile]
        for slot in range(far_slots):
            total = total + jnp.dot(
                scaled[tile * far_slots + slot],
                kernel_half[tile, slot],
                preferred_element_type=jnp.float32,
            )
        raw[:, pl.ds(pl.multiple_of(tile * size, size), size)] = total / degree[tile]
        return carry

    lax.fori_loop(0, tiles, one_tile, 0, unroll=2)
    gram[...] = nt_dot(raw[...], raw[...], lax.Precision.HIGHEST)


def far_apply(lower_inverse, far, inverse, degree, kernel_half, partial):
    tiles, columns, size = partial.shape
    return pl.pallas_call(
        functools.partial(far_apply_body, tiles),
        out_shape=(
            jax.ShapeDtypeStruct((columns, tiles * size), jnp.float32),
            jax.ShapeDtypeStruct((columns, columns), jnp.float32),
        ),
        in_specs=[VMEM] * 6,
        out_specs=(VMEM, VMEM),
        scratch_shapes=[pltpu.VMEM(far.shape, jnp.bfloat16)],
        name="far_apply",
    )(lower_inverse, far, inverse, degree, kernel_half, partial)


def exchange(count, peer, me, source, target, send, recv):
    def copy(step, mine):
        other, device = peer(step)
        slot = me if mine else other
        return pltpu.make_async_remote_copy(
            src_ref=source(other),
            dst_ref=target.at[slot],
            send_sem=send.at[other],
            recv_sem=recv.at[slot],
            device_id=device,
            device_id_type=MESH,
        )

    def start(step, carry):
        copy(step, True).start()
        return carry

    def finish(step, carry):
        copy(step, True).wait_send()
        copy(step, False).wait_recv()
        return carry

    lax.fori_loop(1, count, start, 0)
    lax.fori_loop(1, count, finish, 0)


def greet_all(groups):
    barrier = pltpu.get_barrier_semaphore()
    for count, peer in groups:

        def greet(step, carry):
            pl.semaphore_signal(barrier, inc=1, device_id=peer(step)[1], device_id_type=MESH)
            return carry

        lax.fori_loop(1, count, greet, 0)
    pl.semaphore_wait(barrier, sum(count - 1 for count, _ in groups))


def reduce_body(nz, ny, local, out, parts_w, parts_y, parts_z, stage, sw, rw, sy, ry, sz, rz, sa, ra):
    row = lax.axis_index("rows")
    y = lax.axis_index("grp")
    w = row % PLANE
    z = row // PLANE

    def peer_w(step):
        other = (w + step) % PLANE
        return other, (z * PLANE + other, y)

    def peer_y(step):
        other = (y + step) % ny
        return other, (row, other)

    def peer_z(step):
        other = (z + step) % nz
        return other, (other * PLANE + w, y)

    greet_all(((PLANE, peer_w), (ny, peer_y), (nz, peer_z)))
    exchange(PLANE, peer_w, w, lambda other: local.at[other], parts_w, sw, rw)
    parts_w[w] = local[w]
    stage[0] = jnp.sum(parts_w[...], axis=0)
    exchange(ny, peer_y, y, lambda other: stage.at[0], parts_y, sy, ry)
    parts_y[y] = stage[0]
    stage[1] = jnp.sum(parts_y[...], axis=0)
    exchange(nz, peer_z, z, lambda other: stage.at[1], parts_z, sz, rz)
    parts_z[z] = stage[1]
    stage[2] = jnp.sum(parts_z[...], axis=0)
    exchange(PLANE, peer_w, w, lambda other: stage.at[2], out, sa, ra)
    out[w] = stage[2]


def request_body(nz, wanted, got, parts, sw, rw, sz, rz):
    row = lax.axis_index("rows")
    y = lax.axis_index("grp")
    w = row % PLANE
    z = row // PLANE

    def peer_w(step):
        other = (w + step) % PLANE
        return other, (z * PLANE + other, y)

    def peer_z(step):
        other = (z + step) % nz
        return other, (other * PLANE + w, y)

    greet_all(((PLANE, peer_w), (nz, peer_z)))
    exchange(PLANE, peer_w, w, lambda other: wanted.at[other], parts, sw, rw)
    parts[w] = wanted[w]
    exchange(nz, peer_z, z, lambda other: parts, got, sz, rz)
    got[z] = parts[...]


def swap_requests(wanted):
    nrows = wanted.shape[0]
    nz = nrows // PLANE
    dma = pltpu.SemaphoreType.DMA
    sent = jnp.pad(wanted.reshape(nz, PLANE).T, ((0, 0), (0, 128 - nz)))[:, None, :]
    got = pl.pallas_call(
        functools.partial(request_body, nz),
        out_shape=jax.ShapeDtypeStruct((nz,) + sent.shape, sent.dtype),
        in_specs=[VMEM],
        out_specs=VMEM,
        scratch_shapes=[
            pltpu.VMEM(sent.shape, sent.dtype),
            dma((PLANE,)),
            dma((PLANE,)),
            dma((nz,)),
            dma((nz,)),
        ],
        compiler_params=pltpu.CompilerParams(collective_id=1, has_side_effects=True),
        name="swap_requests",
    )(sent)
    z = lax.axis_index("rows") // PLANE
    return lax.dynamic_index_in_dim(got, z, axis=3, keepdims=False).reshape(nrows)


def total_gram(gram):
    columns = gram.shape[0]
    height = columns // PLANE
    ny = lax.axis_size("grp")
    nz = lax.axis_size("rows") // PLANE
    chunk = (height, columns)
    dma = pltpu.SemaphoreType.DMA
    out = pl.pallas_call(
        functools.partial(reduce_body, nz, ny),
        out_shape=jax.ShapeDtypeStruct((PLANE,) + chunk, jnp.float32),
        in_specs=[VMEM],
        out_specs=VMEM,
        scratch_shapes=[
            pltpu.VMEM((PLANE,) + chunk, jnp.float32),
            pltpu.VMEM((ny,) + chunk, jnp.float32),
            pltpu.VMEM((nz,) + chunk, jnp.float32),
            pltpu.VMEM((3,) + chunk, jnp.float32),
            dma((PLANE,)),
            dma((PLANE,)),
            dma((ny,)),
            dma((ny,)),
            dma((nz,)),
            dma((nz,)),
            dma((PLANE,)),
            dma((PLANE,)),
        ],
        compiler_params=pltpu.CompilerParams(collective_id=0, has_side_effects=True),
        name="gram_reduce",
    )(gram.reshape((PLANE,) + chunk))
    return out.reshape(columns, columns)


def exchange_tiles(tiles, requested, owner):
    sent = jnp.take(tiles, requested, axis=0, mode="clip")
    got = lax.all_to_all(sent, "rows", split_axis=0, concat_axis=0, tiled=True)
    return jnp.take(got, owner, axis=0, mode="clip")


def shards(features, length_scale, prior, partners, counts, projection):
    tiles, slots = partners.shape[1:]
    size = features.shape[1] // tiles
    columns = projection.shape[1]
    nrows = lax.axis_size("rows")
    device_index = lax.axis_index("rows")
    own_rows = features[0].reshape(tiles, size, features.shape[2])
    own_side = jnp.stack(
        [length_scale[0].reshape(tiles, size), prior[0].reshape(tiles, size)], axis=1
    )
    lists = partners[0]
    far_tiles = lists[:, NEAR:].reshape(-1)
    owner = far_tiles // tiles
    hits = owner[:, None] == jnp.arange(nrows, dtype=jnp.int32)[None, :]
    wanted = jnp.sum(jnp.where(hits, (far_tiles % tiles)[:, None], 0), axis=0)
    requested = swap_requests(wanted)
    table = (lists - device_index * tiles).reshape(-1)

    far = exchange_tiles(jnp.concatenate([own_rows, own_side], axis=1), requested, owner)
    side = own_side.astype(jnp.float32)
    own_band, own_prior = side[:, 0:1, :], side[:, 1:2, :]
    directions = projection.T
    near_half, near_density, norms = near_kernel(table, counts[0], own_rows, own_band, slots)
    far_half, own_inverse = far_kernel(
        counts[0], own_rows, own_band, far, norms, near_density, slots
    )
    far_inverse = exchange_tiles(own_inverse.astype(jnp.bfloat16), requested, owner)
    far_inverse = far_inverse.astype(jnp.float32)
    near_part = near_walk(table, own_rows, own_prior, own_inverse, directions, near_half, slots)
    raw, raw_half, degree, gram = far_walk(
        far, far_inverse, directions, far_half, near_part
    )
    far_raw = exchange_tiles(raw_half, requested, owner)
    gram = total_gram(gram)
    total_rows = nrows * lax.axis_size("grp") * tiles * size
    basis, near_second, lower_inverse = near_apply(
        table, gram, raw, own_inverse, near_half, slots, total_rows
    )
    second_raw, second_gram = far_apply(
        lower_inverse, far_raw, far_inverse, degree, far_half, near_second
    )
    embedding = finish(total_gram(second_gram), second_raw, total_rows)
    return basis[None], embedding[None]


def solution(mesh):
    in_specs = (
        P("grp", "rows", None),
        P("grp", "rows"),
        P("grp", "rows"),
        P("grp", "rows", None),
        P("grp", "rows"),
        P(),
    )
    out_specs = (P("grp", None, "rows"), P("grp", None, "rows"))
    return jax.shard_map(shards, mesh=mesh, in_specs=in_specs, out_specs=out_specs, check_vma=False)
```

```python
import functools

import jax
import jax.numpy as jnp
from jax import lax
from jax.experimental import pallas as pl
from jax.experimental.pallas import tpu as pltpu
from jax.sharding import PartitionSpec as P

NEAR = 13
PLANE = 8
MESH = pl.DeviceIdType.MESH
VMEM = pl.BlockSpec(memory_space=pltpu.VMEM)
SMEM = pl.BlockSpec(memory_space=pltpu.SMEM)


def nt_dot(left, right, precision=None):
    return lax.dot_general(
        left,
        right,
        (((1,), (1,)), ((), ())),
        precision=precision,
        preferred_element_type=jnp.float32,
    )


def load_norm(rows):
    wide = rows.astype(jnp.float32)
    norm = jnp.sum(wide * wide, axis=1, keepdims=True)
    return jnp.broadcast_to(-norm, (rows.shape[0], rows.shape[0]))


def column_band(row):
    return jnp.transpose(jnp.broadcast_to(row, (row.shape[1], row.shape[1])))


def kernel_value(rows, norm, band, doubled, own_norm, own_band):
    level = jnp.minimum(nt_dot(rows, doubled) + (norm + own_norm), 0.0)
    return jnp.exp(level / (band + own_band))


def fold_rows(value):
    return jnp.sum(value.reshape(value.shape[0] // 8, 8, value.shape[1]), axis=0)


def near_kernel_body(
    tiles, slots, table, counts, pool, band, kernel_half, density, norm_a, norm_b, band_b
):
    size = pool.shape[1]

    def prepare(index, carry):
        wide = load_norm(pool[index])
        norm_b[index] = wide
        band_b[index] = column_band(band[index])
        norm_a[index] = jnp.transpose(wide)[0:1, :]
        return carry

    lax.fori_loop(0, tiles, prepare, 0)

    def one_tile(tile, carry):
        doubled = pool[tile] * jnp.bfloat16(2)
        own_norm = norm_a[tile]
        own_band = band[tile]
        live = counts[tile]
        total = jnp.zeros((8, size), jnp.float32)
        for slot in range(NEAR):
            index = table[tile * slots + slot]
            value = kernel_value(
                pool[index], norm_b[index], band_b[index], doubled, own_norm, own_band
            )
            if slot == NEAR - 1:
                value = jnp.where(slot < live, value, 0.0)
            kernel_half[tile, slot] = value.astype(jnp.bfloat16)
            total = total + fold_rows(value)
        density[tile] = jnp.sum(total, axis=0, keepdims=True)
        return carry

    lax.fori_loop(0, tiles, one_tile, 0)


def near_kernel(table, counts, pool, band, slots):
    tiles, size, _ = pool.shape
    return pl.pallas_call(
        functools.partial(near_kernel_body, tiles, slots),
        out_shape=(
            jax.ShapeDtypeStruct((tiles, NEAR, size, size), jnp.bfloat16),
            jax.ShapeDtypeStruct((tiles, 1, size), jnp.float32),
            jax.ShapeDtypeStruct((tiles, 1, size), jnp.float32),
        ),
        in_specs=[SMEM, SMEM, VMEM, VMEM],
        out_specs=(VMEM, VMEM, VMEM),
        scratch_shapes=[pltpu.VMEM((tiles, size, size), jnp.float32)] * 2,
        cost_estimate=cost(tiles * NEAR * size * size, 400),
        name="near_kernel",
    )(table, counts, pool, band)


def far_kernel_body(tiles, slots, counts, pool, band, far, norm_a, near, kernel_half, inverse):
    far_slots = slots - NEAR
    size = pool.shape[1]

    def one_tile(tile, carry):
        doubled = pool[tile] * jnp.bfloat16(2)
        live = counts[tile]
        total = jnp.zeros((8, pool.shape[1]), jnp.float32)
        for slot in range(far_slots):
            index = tile * far_slots + slot
            rows = far[index, 0:size, :]
            value = kernel_value(
                rows,
                load_norm(rows),
                column_band(far[index, size : size + 1, :].astype(jnp.float32)),
                doubled,
                norm_a[tile],
                band[tile],
            )
            value = jnp.where(slot + NEAR < live, value, 0.0)
            kernel_half[tile, slot] = value.astype(jnp.bfloat16)
            total = total + fold_rows(value)
        inverse[tile] = 1.0 / (near[tile] + jnp.sum(total, axis=0, keepdims=True))
        return carry

    lax.fori_loop(0, tiles, one_tile, 0, unroll=2)


def far_kernel(counts, pool, band, far, norm_a, near, slots):
    tiles, size, _ = pool.shape
    return pl.pallas_call(
        functools.partial(far_kernel_body, tiles, slots),
        out_shape=(
            jax.ShapeDtypeStruct((tiles, slots - NEAR, size, size), jnp.bfloat16),
            jax.ShapeDtypeStruct((tiles, 1, size), jnp.float32),
        ),
        in_specs=[SMEM] + [VMEM] * 5,
        out_specs=(VMEM, VMEM),
        name="far_kernel",
    )(counts, pool, band, far, norm_a, near)


def cost(flops, scale):
    return pl.CostEstimate(flops=flops * scale, bytes_accessed=flops * 4, transcendentals=flops)


def scale_start(projection, rows, prior, inv):
    start = nt_dot(projection, rows)
    scaled = (start * (prior * inv)).astype(jnp.bfloat16)
    high = inv.astype(jnp.bfloat16).astype(jnp.float32)
    row = lax.broadcasted_iota(jnp.int32, (16, inv.shape[1]), 0)
    extra = jnp.where(row == 0, high, jnp.where(row == 1, inv - high, 0.0))
    return scaled, extra.astype(jnp.bfloat16)


def near_walk_body(
    tiles, slots, table, pool, prior, inverse, projection, kernel_half, partial, scaled
):
    columns = projection.shape[0]

    def prepare(index, carry):
        main, extra = scale_start(projection[...], pool[index], prior[index], inverse[index])
        scaled[index, 0:columns, :] = main
        scaled[index, columns : columns + 16, :] = extra
        return carry

    lax.fori_loop(0, tiles, prepare, 0, unroll=2)

    def one_tile(tile, carry):
        total = jnp.zeros(partial.shape[1:], jnp.float32)
        for slot in range(NEAR):
            total = total + jnp.dot(
                scaled[table[tile * slots + slot]],
                kernel_half[tile, slot],
                preferred_element_type=jnp.float32,
            )
        partial[tile] = total
        return carry

    lax.fori_loop(0, tiles, one_tile, 0)


def near_walk(table, pool, prior, inverse, projection, kernel_half, slots):
    tiles, _, size, _ = kernel_half.shape
    height = projection.shape[0] + 16
    return pl.pallas_call(
        functools.partial(near_walk_body, tiles, slots),
        out_shape=jax.ShapeDtypeStruct((tiles, height, size), jnp.float32),
        in_specs=[SMEM] + [VMEM] * 5,
        out_specs=VMEM,
        scratch_shapes=[pltpu.VMEM((tiles, height, size), jnp.bfloat16)],
        cost_estimate=cost(tiles * NEAR * size * size, 160),
        name="near_walk",
    )(table, pool, prior, inverse, projection, kernel_half)


def far_walk_body(
    tiles, far, inverse, projection, kernel_half, partial, raw, half, degree, gram, scaled
):
    size = far.shape[2]
    columns = projection.shape[0]
    far_slots = kernel_half.shape[1]
    gram[...] = jnp.zeros_like(gram)

    def prepare(index, carry):
        main, extra = scale_start(
            projection[...],
            far[index, 0:size, :],
            far[index, size + 1 : size + 2, :].astype(jnp.float32),
            inverse[index],
        )
        scaled[index, 0:columns, :] = main
        scaled[index, columns : columns + 16, :] = extra
        return carry

    lax.fori_loop(0, far.shape[0], prepare, 0, unroll=4)

    def one_tile(tile, carry):
        total = partial[tile]
        for slot in range(far_slots):
            total = total + jnp.dot(
                scaled[tile * far_slots + slot],
                kernel_half[tile, slot],
                preferred_element_type=jnp.float32,
            )
        below = total[columns : columns + 1] + total[columns + 1 : columns + 2]
        degree[tile] = below
        value = total[0:columns] / below
        raw[:, pl.ds(pl.multiple_of(tile * size, size), size)] = value
        half[tile] = value.astype(jnp.bfloat16)
        return carry

    lax.fori_loop(0, tiles, one_tile, 0, unroll=2)
    gram[...] = nt_dot(raw[...], raw[...], lax.Precision.HIGHEST)


def far_walk(far, inverse, projection, kernel_half, partial):
    tiles, _, size, _ = kernel_half.shape
    columns = projection.shape[0]
    return pl.pallas_call(
        functools.partial(far_walk_body, tiles),
        out_shape=(
            jax.ShapeDtypeStruct((columns, tiles * size), jnp.float32),
            jax.ShapeDtypeStruct((tiles, columns, size), jnp.bfloat16),
            jax.ShapeDtypeStruct((tiles, 1, size), jnp.float32),
            jax.ShapeDtypeStruct((columns, columns), jnp.float32),
        ),
        in_specs=[VMEM] * 5,
        out_specs=(VMEM,) * 4,
        scratch_shapes=[pltpu.VMEM((far.shape[0], columns + 16, size), jnp.bfloat16)],
        name="far_walk",
    )(far, inverse, projection, kernel_half, partial)


def lower_inverse_of(gram, total_rows):
    count = gram.shape[0]
    row = lax.broadcasted_iota(jnp.int32, (count, 2 * count), 0)
    lane = lax.broadcasted_iota(jnp.int32, (count, 2 * count), 1)
    identity = jnp.where(row == lane, 1.0, 0.0)[:, 0:count]
    work = jnp.concatenate([identity, gram * (1.0 / total_rows)], axis=1)
    for step in range(count - 1):
        at = count + step
        factor = work[:, at : at + 1] / work[step : step + 1, at : at + 1]
        below = jnp.where(row[:, 0:1] > step, factor, 0.0)
        work = work - below * work[step : step + 1, :]
    pivots = jnp.sum(jnp.where(lane == row + count, work, 0.0), axis=1, keepdims=True)
    return work[:, 0:count] / jnp.sqrt(pivots)


def finish_body(total_rows, gram, raw, basis):
    basis[...] = jnp.dot(
        lower_inverse_of(gram[...], total_rows),
        raw[...],
        precision=lax.Precision.HIGHEST,
        preferred_element_type=jnp.float32,
    )


def finish(gram, raw, total_rows):
    return pl.pallas_call(
        functools.partial(finish_body, total_rows),
        out_shape=jax.ShapeDtypeStruct(raw.shape, jnp.float32),
        in_specs=[VMEM, VMEM],
        out_specs=VMEM,
        name="finish",
    )(gram, raw)


def near_apply_body(
    tiles, slots, total_rows, table, gram, raw, inverse, kernel_half, basis, partial, lower, scaled
):
    size = inverse.shape[2]
    lower[...] = lower_inverse_of(gram[...], total_rows)
    value = jnp.dot(
        lower[...],
        raw[...],
        precision=lax.Precision.HIGHEST,
        preferred_element_type=jnp.float32,
    )
    basis[...] = value
    for tile in range(tiles):
        part = value[:, tile * size : (tile + 1) * size]
        scaled[tile] = (part * inverse[tile]).astype(jnp.bfloat16)

    def one_tile(tile, carry):
        total = jnp.zeros(partial.shape[1:], jnp.float32)
        for slot in range(NEAR):
            total = total + jnp.dot(
                scaled[table[tile * slots + slot]],
                kernel_half[tile, slot],
                preferred_element_type=jnp.float32,
            )
        partial[tile] = total
        return carry

    lax.fori_loop(0, tiles, one_tile, 0, unroll=2)


def near_apply(table, gram, raw, inverse, kernel_half, slots, total_rows):
    tiles, _, size, _ = kernel_half.shape
    columns = raw.shape[0]
    return pl.pallas_call(
        functools.partial(near_apply_body, tiles, slots, total_rows),
        out_shape=(
            jax.ShapeDtypeStruct(raw.shape, jnp.float32),
            jax.ShapeDtypeStruct((tiles, columns, size), jnp.float32),
            jax.ShapeDtypeStruct(gram.shape, jnp.float32),
        ),
        in_specs=[SMEM] + [VMEM] * 4,
        out_specs=(VMEM, VMEM, VMEM),
        scratch_shapes=[pltpu.VMEM((tiles, columns, size), jnp.bfloat16)],
        cost_estimate=cost(tiles * NEAR * size * size, 128),
        name="near_apply",
    )(table, gram, raw, inverse, kernel_half)


def far_apply_body(tiles, lower_inverse, far, inverse, degree, kernel_half, partial, raw, gram, scaled):
    size = far.shape[2]
    far_slots = kernel_half.shape[1]

    def prepare(index, carry):
        basis = jnp.dot(
            lower_inverse[...],
            far[index].astype(jnp.float32),
            precision=lax.Precision.HIGHEST,
            preferred_element_type=jnp.float32,
        )
        scaled[index] = (basis * inverse[index]).astype(jnp.bfloat16)
        return carry

    lax.fori_loop(0, far.shape[0], prepare, 0, unroll=4)

    def one_tile(tile, carry):
        total = partial[tile]
        for slot in range(far_slots):
            total = total + jnp.dot(
                scaled[tile * far_slots + slot],
                kernel_half[tile, slot],
                preferred_element_type=jnp.float32,
            )
        raw[:, pl.ds(pl.multiple_of(tile * size, size), size)] = total / degree[tile]
        return carry

    lax.fori_loop(0, tiles, one_tile, 0, unroll=2)
    gram[...] = nt_dot(raw[...], raw[...], lax.Precision.HIGHEST)


def far_apply(lower_inverse, far, inverse, degree, kernel_half, partial):
    tiles, columns, size = partial.shape
    return pl.pallas_call(
        functools.partial(far_apply_body, tiles),
        out_shape=(
            jax.ShapeDtypeStruct((columns, tiles * size), jnp.float32),
            jax.ShapeDtypeStruct((columns, columns), jnp.float32),
        ),
        in_specs=[VMEM] * 6,
        out_specs=(VMEM, VMEM),
        scratch_shapes=[pltpu.VMEM(far.shape, jnp.bfloat16)],
        name="far_apply",
    )(lower_inverse, far, inverse, degree, kernel_half, partial)


def exchange(count, peer, me, source, target, send, recv):
    def copy(step, mine):
        other, device = peer(step)
        slot = me if mine else other
        return pltpu.make_async_remote_copy(
            src_ref=source(other),
            dst_ref=target.at[slot],
            send_sem=send.at[other],
            recv_sem=recv.at[slot],
            device_id=device,
            device_id_type=MESH,
        )

    def start(step, carry):
        copy(step, True).start()
        return carry

    def finish(step, carry):
        copy(step, True).wait_send()
        copy(step, False).wait_recv()
        return carry

    lax.fori_loop(1, count, start, 0)
    lax.fori_loop(1, count, finish, 0)


def greet_all(groups):
    barrier = pltpu.get_barrier_semaphore()
    for count, peer in groups:

        def greet(step, carry):
            pl.semaphore_signal(barrier, inc=1, device_id=peer(step)[1], device_id_type=MESH)
            return carry

        lax.fori_loop(1, count, greet, 0)
    pl.semaphore_wait(barrier, sum(count - 1 for count, _ in groups))


def reduce_body(nz, ny, local, out, parts_w, parts_y, parts_z, stage, sw, rw, sy, ry, sz, rz, sa, ra):
    row = lax.axis_index("rows")
    y = lax.axis_index("grp")
    w = row % PLANE
    z = row // PLANE

    def peer_w(step):
        other = (w + step) % PLANE
        return other, (z * PLANE + other, y)

    def peer_y(step):
        other = (y + step) % ny
        return other, (row, other)

    def peer_z(step):
        other = (z + step) % nz
        return other, (other * PLANE + w, y)

    greet_all(((PLANE, peer_w), (ny, peer_y), (nz, peer_z)))
    exchange(PLANE, peer_w, w, lambda other: local.at[other], parts_w, sw, rw)
    parts_w[w] = local[w]
    stage[0] = jnp.sum(parts_w[...], axis=0)
    exchange(ny, peer_y, y, lambda other: stage.at[0], parts_y, sy, ry)
    parts_y[y] = stage[0]
    stage[1] = jnp.sum(parts_y[...], axis=0)
    exchange(nz, peer_z, z, lambda other: stage.at[1], parts_z, sz, rz)
    parts_z[z] = stage[1]
    stage[2] = jnp.sum(parts_z[...], axis=0)
    exchange(PLANE, peer_w, w, lambda other: stage.at[2], out, sa, ra)
    out[w] = stage[2]


def request_body(nz, wanted, got, parts, sw, rw, sz, rz):
    row = lax.axis_index("rows")
    y = lax.axis_index("grp")
    w = row % PLANE
    z = row // PLANE

    def peer_w(step):
        other = (w + step) % PLANE
        return other, (z * PLANE + other, y)

    def peer_z(step):
        other = (z + step) % nz
        return other, (other * PLANE + w, y)

    greet_all(((PLANE, peer_w), (nz, peer_z)))
    exchange(PLANE, peer_w, w, lambda other: wanted.at[other], parts, sw, rw)
    parts[w] = wanted[w]
    exchange(nz, peer_z, z, lambda other: parts, got, sz, rz)
    got[z] = parts[...]


def swap_requests(wanted):
    nrows = wanted.shape[0]
    nz = nrows // PLANE
    dma = pltpu.SemaphoreType.DMA
    sent = jnp.pad(wanted.reshape(nz, PLANE).T, ((0, 0), (0, 128 - nz)))[:, None, :]
    got = pl.pallas_call(
        functools.partial(request_body, nz),
        out_shape=jax.ShapeDtypeStruct((nz,) + sent.shape, sent.dtype),
        in_specs=[VMEM],
        out_specs=VMEM,
        scratch_shapes=[
            pltpu.VMEM(sent.shape, sent.dtype),
            dma((PLANE,)),
            dma((PLANE,)),
            dma((nz,)),
            dma((nz,)),
        ],
        compiler_params=pltpu.CompilerParams(collective_id=1, has_side_effects=True),
        name="swap_requests",
    )(sent)
    z = lax.axis_index("rows") // PLANE
    return lax.dynamic_index_in_dim(got, z, axis=3, keepdims=False).reshape(nrows)


def total_gram(gram):
    columns = gram.shape[0]
    height = columns // PLANE
    ny = lax.axis_size("grp")
    nz = lax.axis_size("rows") // PLANE
    chunk = (height, columns)
    dma = pltpu.SemaphoreType.DMA
    out = pl.pallas_call(
        functools.partial(reduce_body, nz, ny),
        out_shape=jax.ShapeDtypeStruct((PLANE,) + chunk, jnp.float32),
        in_specs=[VMEM],
        out_specs=VMEM,
        scratch_shapes=[
            pltpu.VMEM((PLANE,) + chunk, jnp.float32),
            pltpu.VMEM((ny,) + chunk, jnp.float32),
            pltpu.VMEM((nz,) + chunk, jnp.float32),
            pltpu.VMEM((3,) + chunk, jnp.float32),
            dma((PLANE,)),
            dma((PLANE,)),
            dma((ny,)),
            dma((ny,)),
            dma((nz,)),
            dma((nz,)),
            dma((PLANE,)),
            dma((PLANE,)),
        ],
        compiler_params=pltpu.CompilerParams(collective_id=0, has_side_effects=True),
        name="gram_reduce",
    )(gram.reshape((PLANE,) + chunk))
    return out.reshape(columns, columns)


def exchange_tiles(tiles, requested, owner):
    sent = jnp.take(tiles, requested, axis=0, mode="clip")
    got = lax.all_to_all(sent, "rows", split_axis=0, concat_axis=0, tiled=True)
    return jnp.take(got, owner, axis=0, mode="clip")


def shards(features, length_scale, prior, partners, counts, projection):
    tiles, slots = partners.shape[1:]
    size = features.shape[1] // tiles
    columns = projection.shape[1]
    nrows = lax.axis_size("rows")
    device_index = lax.axis_index("rows")
    own_rows = features[0].reshape(tiles, size, features.shape[2])
    own_side = jnp.stack(
        [length_scale[0].reshape(tiles, size), prior[0].reshape(tiles, size)], axis=1
    )
    lists = partners[0]
    far_tiles = lists[:, NEAR:].reshape(-1)
    owner = far_tiles // tiles
    hits = owner[:, None] == jnp.arange(nrows, dtype=jnp.int32)[None, :]
    wanted = jnp.sum(jnp.where(hits, (far_tiles % tiles)[:, None], 0), axis=0)
    requested = swap_requests(wanted)
    table = (lists - device_index * tiles).reshape(-1)

    far = exchange_tiles(jnp.concatenate([own_rows, own_side], axis=1), requested, owner)
    side = own_side.astype(jnp.float32)
    own_band, own_prior = side[:, 0:1, :], side[:, 1:2, :]
    directions = projection.T
    near_half, near_density, norms = near_kernel(table, counts[0], own_rows, own_band, slots)
    far_half, own_inverse = far_kernel(
        counts[0], own_rows, own_band, far, norms, near_density, slots
    )
    far_inverse = exchange_tiles(own_inverse.astype(jnp.bfloat16), requested, owner)
    far_inverse = far_inverse.astype(jnp.float32)
    near_part = near_walk(table, own_rows, own_prior, own_inverse, directions, near_half, slots)
    raw, raw_half, degree, gram = far_walk(
        far, far_inverse, directions, far_half, near_part
    )
    far_raw = exchange_tiles(raw_half, requested, owner)
    gram = total_gram(gram)
    total_rows = nrows * lax.axis_size("grp") * tiles * size
    basis, near_second, lower_inverse = near_apply(
        table, gram, raw, own_inverse, near_half, slots, total_rows
    )
    second_raw, second_gram = far_apply(
        lower_inverse, far_raw, far_inverse, degree, far_half, near_second
    )
    embedding = finish(total_gram(second_gram), second_raw, total_rows)
    return basis[None], embedding[None]


def solution(mesh):
    in_specs = (
        P("grp", "rows", None),
        P("grp", "rows"),
        P("grp", "rows"),
        P("grp", "rows", None),
        P("grp", "rows"),
        P(),
    )
    out_specs = (P("grp", None, "rows"), P("grp", None, "rows"))
    return jax.shard_map(shards, mesh=mesh, in_specs=in_specs, out_specs=out_specs, check_vma=False)
```
